256 devices in a mesh: expert: 32 (over y, z_lo, core), fsdp: 4 (over x), replica: 2 (over z_hi).
Axes of the slice: x: 4, y: 4, z: 8 (z_hi: 2, z_lo: 4; z = z_hi * 4 + z_lo), core: 2. Of those that a mesh axis runs over, the one named last changes fastest.
Arguments:
- out_grad: bfloat16 [32768, 2048], P(('expert', 'fsdp', 'replica')), may hold values from -6 to 6
- hidden_saved: bfloat16 [32768, 8, 768], P(('expert', 'fsdp', 'replica')), may hold values from -6 to 6
- gate_probs: float32 [32768, 8], P(('expert', 'fsdp', 'replica')), may hold values from 0.05 to 0.5
- expert_ids: int32 [32768, 8], P(('expert', 'fsdp', 'replica')), may hold values from 0 to 63, all different within a row; in each aligned block of 128 rows (0 to 127, 128 to 255, ...) at most 32 rows name the same one
- weight_q: bfloat16 [64, 768, 2048], P('expert', 'fsdp'), may hold values from -0.21875 to 0.21875
- weight_exp: int32 [64, 768, 16], P('expert', 'fsdp'), may hold values from -1 to 1
- master: float32 [64, 768, 2048], P('expert', ('fsdp', 'replica')), may hold values from -0.21875 to 0.21875
- moment1: bfloat16 [64, 768, 2048], P('expert', ('fsdp', 'replica')), may hold values from -6 to 6
- moment2: bfloat16 [64, 768, 2048], P('expert', ('fsdp', 'replica')), may hold values from 0.099609375 to 10
Outputs:
- hidden_grad: bfloat16 [32768, 8, 768], P(('expert', 'fsdp', 'replica'))
- gate_grad: float32 [32768, 8], P(('expert', 'fsdp', 'replica'))
- master_new: float32 [64, 768, 2048], P('expert', ('fsdp', 'replica'))
- moment1_new: bfloat16 [64, 768, 2048], P('expert', ('fsdp', 'replica'))
- moment2_new: bfloat16 [64, 768, 2048], P('expert', ('fsdp', 'replica'))
The draws below stay inside these ranges and needn't reach their ends.
Inputs may be any that keep to these rules, and one draw needn't show every extreme that they name: `expert_ids`: each token names 8 different experts; the tokens of one device name any one expert at most 32 times.
All inputs are finite; a program needn't handle non-finite values.
Results may differ from the reference program's by a relative error of at most 0.0051.
Values may be sent and summed in bfloat16 or wider, within the bound.
A program may use at most 128 MiB of HBM per device.

```python
import math
import jax
import jax.numpy as jnp
import numpy as np
from jax import lax

D = 2048
FF = 768
TOP = 8
QB = 128
TOK_DEV = 128
EXPERTS = 64
TOKENS = 32768
CAP = 32
N_EXPERT = 32
N_FSDP = 4
N_REPLICA = 2


def set_ends(result, stream_key, low, largest):
    shape = result.shape
    spot = [jax.random.randint(jax.random.fold_in(stream_key, axis), (), 0, shape[axis]) for axis in range(len(shape))]
    result = result.at[tuple(spot)].set(low)
    longest = shape.index(max(shape))
    spot[longest] = (spot[longest] + 1) % shape[longest]
    return result.at[tuple(spot)].set(largest)


def block_levels(stream_key, extent, shards, low, largest):
    def one(dim, shards_of):
        steps = jax.random.uniform(jax.random.fold_in(jax.random.fold_in(stream_key, 6), dim), (shards_of,), jnp.float32, low / len(shards), largest / len(shards))
        return jnp.repeat(jnp.exp(steps), extent[dim] // shards_of).reshape((-1,) + (1,) * (len(extent) - dim - 1))

    level = one(*shards[0])
    for cut in shards[1:]:
        level = level * one(*cut)
    return level


def routed_block(own_key, own, number, rows, number_of, top, bound, slope):
    ranking = jax.random.permutation(own_key, number_of)
    heavy_load, common = shares(number_of, rows * top, bound, slope, True), shares(number_of, rows * top, bound, slope, False)
    places = jnp.arange(number_of)

    def named(sizes, turn):
        used = int((sizes > 0).sum())
        fixed = max(1, used // 4)
        moved = fixed + (places - fixed + turn * (used - fixed)) % max(1, number_of - fixed)
        return jnp.zeros((number_of,), jnp.int32).at[ranking[jnp.where(places < fixed, places, moved)]].set(jnp.asarray(sizes, jnp.int32))

    sizes = jnp.where(number % 4 == 0, named(heavy_load, number // 4), named(common, number - number // 4 - 1))
    mixed = jax.random.permutation(jax.random.fold_in(own, 3), number_of)
    giver, taker = mixed[0:number_of // 2 * 2:2], mixed[1:number_of // 2 * 2:2]
    room = jnp.minimum(sizes[giver] - 1, bound - sizes[taker]) // 2
    room = jnp.where((giver == ranking[0]) | (taker == ranking[0]) | (sizes[taker] == 0), 0, jnp.maximum(room, 0))
    moved = jax.random.randint(jax.random.fold_in(own, 4), (number_of // 2,), 0, 1 << 20) % (room + 1)
    sizes = sizes.at[giver].add(-moved).at[taker].add(moved)
    members = jnp.searchsorted(jnp.cumsum(sizes), jnp.arange(rows * top), side="right").astype(jnp.int32)
    listing = members.reshape(top, rows).T
    listing = listing[jax.random.permutation(jax.random.fold_in(own, 1), rows)]
    turn = jax.random.randint(jax.random.fold_in(own, 2), (rows, 1), 0, top)
    return jnp.take_along_axis(listing, (jnp.arange(top)[None, :] + turn) % top, axis=1)


def shares(amount, total, reach, skew, full):
    loads = [(1 << 20) // math.isqrt(standing ** skew) + 1 for standing in range(1, amount + 1)]
    largest = reach if full else min(reach, max(-(-total // amount), total * loads[0] // sum(loads)))
    least = 1 if total - largest >= amount - 1 else 0
    given, spare = [largest] + [least] * (amount - 1), total - largest - least * (amount - 1)
    while spare > 0:
        candidates = [i for i in range(1, amount) if given[i] < largest] or [i for i in range(1, amount) if given[i] < reach]
        mass, budget = sum([loads[i] for i in candidates]), spare
        for i in candidates:
            more = min(reach - given[i], max(1, budget * loads[i] // mass), spare)
            given[i] = given[i] + more
            spare = spare - more
    return np.array(given)


def scatter_about(key, dims, deviation, reach, cuts=(), kind=jnp.bfloat16):
    values = deviation * jax.random.normal(key, dims, jnp.float32)
    if cuts:
        values = values * block_levels(key, dims, cuts, -0.22, 0.18)
    return jnp.clip(values, -reach, reach).astype(kind)


def setup_inputs(seed: int = 0) -> dict:
    key_list = jax.random.split(jax.random.key(seed), 10)
    out_grad = scatter_about(key_list[0], (TOKENS, D), 1.0, 6.0, ((0, 256),))
    hidden_saved = scatter_about(key_list[1], (TOKENS, TOP, FF), 1.0, 6.0, ((0, 256),))
    gate_probs = jnp.clip(jnp.exp(math.log(0.5) - 2.3025851 * jax.random.uniform(key_list[2], (TOKENS, TOP), jnp.float32) ** block_levels(key_list[2], (TOKENS, TOP), ((0, 256),), -0.2, 0.2)), 0.05, 0.5)
    expert_ids_keys = jax.random.split(jax.random.fold_in(key_list[3], 1), TOKENS // TOK_DEV)
    expert_ids_turns = jax.random.permutation(jax.random.fold_in(key_list[3], 3), TOKENS // TOK_DEV)
    expert_ids = jax.vmap(lambda own, number: routed_block(jax.random.fold_in(key_list[3], 2), own, number, TOK_DEV, EXPERTS, TOP, CAP, 2))(expert_ids_keys, expert_ids_turns).reshape((TOKENS, TOP))
    weight_q = scatter_about(key_list[4], (EXPERTS, FF, D), FF ** -0.5, 0.21875, ((0, 32), (1, 4)))
    weight_exp = set_ends(jax.random.randint(key_list[5], (EXPERTS, FF, D // QB), -1, 2), jax.random.fold_in(key_list[5], 1), -1, 1).astype(jnp.int32)
    master = scatter_about(key_list[6], (EXPERTS, FF, D), FF ** -0.5, 0.21875, ((0, 32), (1, 8)), jnp.float32)
    moment1 = scatter_about(key_list[7], (EXPERTS, FF, D), 1.0, 6.0, ((0, 32), (1, 8)))
    moment2 = jnp.clip(jnp.exp(math.log(10.0) - 4.609084 * jax.random.uniform(key_list[8], (EXPERTS, FF, D), jnp.float32) ** block_levels(key_list[8], (EXPERTS, FF, D), ((0, 32), (1, 8)), -0.2, 0.2)), 0.099609375, 10.0).astype(jnp.bfloat16)
    return dict(out_grad=out_grad, hidden_saved=hidden_saved, gate_probs=gate_probs, expert_ids=expert_ids, weight_q=weight_q, weight_exp=weight_exp, master=master, moment1=moment1, moment2=moment2)


def reference(out_grad, hidden_saved, gate_probs, expert_ids, weight_q, weight_exp, master, moment1, moment2):
    scales = jnp.exp2(weight_exp.astype(jnp.float32))
    weight = (weight_q.astype(jnp.float32).reshape(EXPERTS, FF, D // QB, QB) * scales[..., None]).reshape(EXPERTS, FF, D).astype(jnp.bfloat16)
    routes = TOKENS * TOP
    weighted = (gate_probs[..., None] * hidden_saved.astype(jnp.float32)).astype(jnp.bfloat16).reshape(routes, FF)
    flat_ids = expert_ids.reshape(-1).astype(jnp.int32)
    sorted_routes = jnp.argsort(flat_ids, stable=True).astype(jnp.int32)
    counts = jnp.bincount(flat_ids, length=EXPERTS).astype(jnp.int32)
    starts = (jnp.cumsum(counts) - counts).astype(jnp.int32)
    max_rows = N_EXPERT * N_FSDP * N_REPLICA * CAP
    padded = jnp.concatenate([sorted_routes, jnp.zeros((max_rows,), jnp.int32)])

    def per_expert(index):
        chosen = lax.dynamic_slice_in_dim(padded, starts[index], max_rows)
        is_valid = jnp.arange(max_rows) < counts[index]
        dy_rows = jnp.where(is_valid[:, None], out_grad[chosen // TOP], jnp.zeros((), jnp.bfloat16))
        h_rows = jnp.where(is_valid[:, None], weighted[chosen], jnp.zeros((), jnp.bfloat16))
        back_rows = jnp.dot(dy_rows, weight[index].T, preferred_element_type=jnp.float32).astype(jnp.bfloat16)
        part_grad = jnp.dot(h_rows.T, dy_rows, preferred_element_type=jnp.float32)
        return (back_rows, part_grad)
    backs, gradient = lax.map(per_expert, jnp.arange(EXPERTS, dtype=jnp.int32))
    position = jnp.zeros((routes,), jnp.int32).at[sorted_routes].set(jnp.arange(routes, dtype=jnp.int32))
    local_pos = position - starts[flat_ids]
    back_route = backs.reshape(EXPERTS * max_rows, FF)[flat_ids * max_rows + local_pos].reshape(TOKENS, TOP, FF)
    back_float = back_route.astype(jnp.float32)
    hidden_grad = (gate_probs[..., None] * back_float).astype(jnp.bfloat16)
    gate_grad = lax.optimization_barrier(jnp.sum(hidden_saved.astype(jnp.float32) * back_float, axis=-1))
    first = 0.9 * moment1.astype(jnp.float32) + 0.1 * gradient
    second = 0.95 * moment2.astype(jnp.float32) + 0.05 * gradient * gradient
    update = first / (1.0 - 0.9 ** 20) / (jnp.sqrt(second / (1.0 - 0.95 ** 20)) + 1e-08) + 0.1 * master
    master_new = master - 0.001 * update
    return (hidden_grad, gate_grad, master_new, first.astype(jnp.bfloat16), second.astype(jnp.bfloat16))
```

```python
import jax
import jax.numpy as jnp
from jax import lax
from jax.experimental import pallas as pl
from jax.experimental.pallas import tpu as pltpu
from jax.sharding import PartitionSpec as P

MESH = pl.DeviceIdType.MESH
NY, NZ, NZL, NX = 4, 8, 4, 4
CAP = 32
ANY = pl.BlockSpec(memory_space=pl.ANY)
VMEM = pl.BlockSpec(memory_space=pltpu.VMEM)


class Place:
    def __init__(self):
        self.own = lax.axis_index("expert")
        self.core = lax.rem(self.own, 2)
        self.y = self.own // (2 * NZL)
        self.z = lax.axis_index("replica") * NZL + lax.rem(self.own // 2, NZL)
        self.x = lax.axis_index("fsdp")
        self.s = 1 - 2 * self.core

    def slot(self, dy, dz, core):
        y = lax.rem(self.y + dy + NY, NY)
        zl = lax.rem(self.z + dz + NZ, NZL)
        return (y * NZL + zl) * 2 + core

    def dev(self, dy, dz, core):
        return {
            "expert": self.slot(dy, dz, core),
            "replica": lax.rem(self.z + dz + NZ, NZ) // NZL,
        }

    def dev_x(self, dx):
        return {"fsdp": lax.rem(self.x + dx + NX, NX)}


def remote(src, dst, ssem, rsem, dev):
    return pltpu.make_async_remote_copy(
        src_ref=src, dst_ref=dst, send_sem=ssem, recv_sem=rsem, device_id=dev, device_id_type=MESH
    )


def peers(p, far):
    out = []
    for dc in (0, 1):
        core = p.core if dc == 0 else 1 - p.core
        for dy in range(NY):
            for kind in range(NZL):
                if dc == 0 and dy == 0 and kind == 0:
                    continue
                dz = (0, 1, far(core), -1)[kind]
                out.append(p.dev(dy, dz, core))
    return out


def dispatch_kernel(
    dy_ref, ws_ref, code_ref, w_ref, rdy_ref, rw_ref, rcode_ref, wf_ref,
    dy_ss, dy_rs, b_ss, b_rs, c_ss, c_rs, w_ss, w_rs, l_sem,
):
    p = Place()
    core, s = p.core, p.s
    half = dy_ref.shape[0] // 2
    sends = []
    count = [0, 0]

    def start(c):
        c.start()
        sends.append(c)

    def part(slot, h):
        return rdy_ref.at[slot, pl.ds(h * half, half)]

    def at(h, a, b):
        return (a, b) if h == 0 else (b, a)

    def send_dy(src, slot, h, dev):
        k = count[h]
        count[h] += 1
        start(remote(src, part(slot, h), dy_ss.at[h, k], dy_rs.at[h, slot], dev))

    def wait_dy(slot, h):
        blk = part(slot, h)
        remote(blk, blk, dy_ss.at[h, 0], dy_rs.at[h, slot], p.dev(1, 0, core)).wait_recv()

    local = [
        pltpu.make_async_copy(w_ref, wf_ref.at[p.x], l_sem.at[0]),
        pltpu.make_async_copy(dy_ref, rdy_ref.at[p.own], l_sem.at[1]),
        pltpu.make_async_copy(ws_ref.at[p.own], rw_ref.at[p.own], l_sem.at[2]),
        pltpu.make_async_copy(code_ref.at[p.own], rcode_ref.at[p.own], l_sem.at[3]),
    ]
    for c in local:
        c.start()

    for i, dx in enumerate((1, -1)):
        start(remote(w_ref, wf_ref.at[p.x], w_ss.at[i], w_rs.at[p.x], p.dev_x(dx)))

    def mine(h):
        return dy_ref.at[pl.ds(h * half, half)]

    for h in (0, 1):
        for d in (1, -1):
            send_dy(mine(h), p.own, h, p.dev(*at(h, d, 0), core))
    for h in (0, 1):
        for d in (1, -1):
            send_dy(mine(h), p.own, h, p.dev(*at(h, 0, d), core))
        send_dy(mine(h), p.own, h, p.dev(0, 0, 1 - core))

    for k, dev in enumerate(peers(p, lambda c: 2 * s)):
        tgt = dev["expert"]
        start(remote(ws_ref.at[tgt], rw_ref.at[p.own], b_ss.at[k], b_rs.at[p.own], dev))
        start(remote(code_ref.at[tgt], rcode_ref.at[p.own], c_ss.at[k], c_rs.at[p.own], dev))

    for h in (0, 1):
        b = p.slot(*at(h, -s, 0), core)
        wait_dy(b, h)
        send_dy(part(b, h), b, h, p.dev(*at(h, s, 0), core))

    for i, a in enumerate((-s, s, -2 * s)):
        for h in (0, 1):
            b = p.slot(*at(h, a, 0), core)
            if i > 0:
                wait_dy(b, h)
            for d in (1, -1):
                send_dy(part(b, h), b, h, p.dev(*at(h, 0, d), core))
            send_dy(part(b, h), b, h, p.dev(0, 0, 1 - core))

    back_x = lax.rem(p.x - s + NX, NX)
    shard = wf_ref.at[back_x]
    remote(shard, shard, w_ss.at[2], w_rs.at[back_x], p.dev_x(s)).wait_recv()
    start(remote(shard, shard, w_ss.at[2], w_rs.at[back_x], p.dev_x(s)))

    for a in (0, -s, s, -2 * s):
        for h in (0, 1):
            b = p.slot(*at(h, a, -s), core)
            wait_dy(b, h)
            send_dy(part(b, h), b, h, p.dev(*at(h, 0, s), core))
            send_dy(part(b, h), b, h, p.dev(0, 0, 1 - core))
    for d in (s, -2 * s):
        for a in (0, -s, s, -2 * s):
            for h in (0, 1):
                b = p.slot(*at(h, a, d), core)
                wait_dy(b, h)
                send_dy(part(b, h), b, h, p.dev(0, 0, 1 - core))

    for dx in (1, 2):
        j = lax.rem(p.x + dx * s + NX + NX, NX)
        blk = wf_ref.at[j]
        remote(blk, blk, w_ss.at[0], w_rs.at[j], p.dev_x(1)).wait_recv()
    for dc in (0, 1):
        c2 = core if dc == 0 else 1 - core
        for dy in range(NY):
            for dz in range(NZL):
                j = p.slot(dy, dz, c2)
                if dc == 1:
                    for h in (0, 1):
                        wait_dy(j, h)
                elif dy == 0 and dz == 0:
                    continue
                a, b = rw_ref.at[j], rcode_ref.at[j]
                remote(a, a, b_ss.at[0], b_rs.at[j], p.dev(1, 0, core)).wait_recv()
                remote(b, b, c_ss.at[0], c_rs.at[j], p.dev(1, 0, core)).wait_recv()
    for c in local:
        c.wait()
    for c in sends:
        c.wait_send()


def dispatch(dy, ws, code, w):
    n, e2c, f = ws.shape
    bf = jnp.bfloat16
    dma = pltpu.SemaphoreType.DMA
    return pl.pallas_call(
        dispatch_kernel,
        out_shape=(
            jax.ShapeDtypeStruct((n,) + dy.shape, bf),
            jax.ShapeDtypeStruct(ws.shape, bf),
            jax.ShapeDtypeStruct(code.shape, jnp.float32),
            jax.ShapeDtypeStruct((NX,) + w.shape, bf),
        ),
        in_specs=[VMEM, ANY, ANY, VMEM],
        out_specs=(ANY, ANY, ANY, ANY),
        scratch_shapes=[
            dma((2, 31)), dma((2, 32)), dma((31,)), dma((32,)), dma((31,)), dma((32,)),
            dma((3,)), dma((4,)), dma((4,)),
        ],
        compiler_params=pltpu.CompilerParams(has_side_effects=True),
        name="dispatch",
    )(dy, ws, code, w)


def giveback_kernel(back_ref, grad_ref, rb_ref, rg_ref, d_ss, d_rs, e_ss, e_rs, l_sem):
    p = Place()
    core = p.core
    sends = []

    def start(c):
        c.start()
        sends.append(c)

    local = [
        pltpu.make_async_copy(back_ref.at[p.own], rb_ref.at[p.own], l_sem.at[0]),
    ]
    for c in local:
        c.start()
    for k, dev in enumerate(peers(p, lambda c: 4 * c - 2)):
        src = back_ref.at[dev["expert"]]
        start(remote(src, rb_ref.at[p.own], d_ss.at[k], d_rs.at[p.own], dev))
    for k, dx in enumerate((1, -1, 2)):
        tgt = lax.rem(p.x + dx + NX, NX)
        start(remote(grad_ref.at[tgt], rg_ref.at[k], e_ss.at[k], e_rs.at[k], p.dev_x(dx)))
    for dc in (0, 1):
        c2 = core if dc == 0 else 1 - core
        for dy in range(NY):
            for dz in range(NZL):
                if dc == 0 and dy == 0 and dz == 0:
                    continue
                j = p.slot(dy, dz, c2)
                a = rb_ref.at[j]
                remote(a, a, d_ss.at[0], d_rs.at[j], p.dev(1, 0, core)).wait_recv()
    for k in range(3):
        a = rg_ref.at[k]
        remote(a, a, e_ss.at[k], e_rs.at[k], p.dev_x(1)).wait_recv()
    for c in local:
        c.wait()
    for c in sends:
        c.wait_send()


def giveback(back, grad):
    dma = pltpu.SemaphoreType.DMA
    bf = jnp.bfloat16
    return pl.pallas_call(
        giveback_kernel,
        out_shape=(
            jax.ShapeDtypeStruct(back.shape, bf),
            jax.ShapeDtypeStruct((NX - 1,) + grad.shape[1:], bf),
        ),
        in_specs=[ANY, ANY],
        out_specs=(ANY, ANY),
        scratch_shapes=[dma((31,)), dma((32,)), dma((3,)), dma((3,)), dma((1,))],
        compiler_params=pltpu.CompilerParams(has_side_effects=True),
        name="giveback",
    )(back, grad)


def prep_kernel(ids_ref, ids_t_ref, w_ref, ws_ref, code_ref, slot_ref):
    experts = code_ref.shape[0]
    routes = ids_ref.shape[1]
    tokens = ids_t_ref.shape[1]
    f32, bf = jnp.float32, jnp.bfloat16

    def ranks(named, n):
        before = lax.broadcasted_iota(jnp.int32, (n, n), 0) < lax.broadcasted_iota(
            jnp.int32, (n, n), 1
        )
        return jnp.dot(named.astype(bf), before.astype(bf), preferred_element_type=f32)

    ids = ids_ref[...]
    named = jnp.where(
        ids == lax.broadcasted_iota(jnp.int32, (experts, routes), 0), 1.0, 0.0
    ).astype(f32)
    rank = jnp.sum(named * ranks(named, routes), axis=0, keepdims=True)
    slot = ids * CAP + rank.astype(jnp.int32)
    slot_ref[...] = slot

    ids_t = ids_t_ref[...]
    named_t = jnp.zeros((experts, tokens), f32)
    for k in range(ids_t_ref.shape[0]):
        named_t += jnp.where(
            ids_t[k : k + 1] == lax.broadcasted_iota(jnp.int32, (experts, tokens), 0), 1.0, 0.0
        )
    code_ref[...] = jnp.where(named_t > 0, ranks(named_t, tokens), -1.0)

    step = 256

    def body(i, _):
        at = pl.multiple_of(i * step, step)
        pick = (slot == lax.broadcasted_iota(jnp.int32, (step, routes), 0) + at).astype(f32)
        ws_ref[pl.ds(at, step)] = jnp.dot(
            pick.astype(bf), w_ref[...], preferred_element_type=f32
        ).astype(bf)
        return 0

    lax.fori_loop(0, ws_ref.shape[0] // step, body, 0)


def prep(ids, ids_t, weighted, experts):
    return pl.pallas_call(
        prep_kernel,
        out_shape=(
            jax.ShapeDtypeStruct((experts * CAP, weighted.shape[1]), jnp.bfloat16),
            jax.ShapeDtypeStruct((experts, ids_t.shape[1]), jnp.float32),
            jax.ShapeDtypeStruct(ids.shape, jnp.int32),
        ),
        in_specs=[VMEM, VMEM, VMEM],
        out_specs=(VMEM, VMEM, VMEM),
        name="prep",
    )(ids, ids_t, weighted)


def combine_kernel(slot_ref, gate_ref, h_ref, rb_ref, hg_ref, gg_ref):
    f32, bf = jnp.float32, jnp.bfloat16
    rows, slots = slot_ref.shape[0], rb_ref.shape[0]
    pick = (slot_ref[...] == lax.broadcasted_iota(jnp.int32, (rows, slots), 1)).astype(f32)
    back = jnp.dot(pick.astype(bf), rb_ref[...], preferred_element_type=f32)
    hg_ref[...] = (gate_ref[...] * back).astype(bf)
    gg_ref[...] = jnp.sum(h_ref[...].astype(f32) * back, axis=1, keepdims=True)


def combine(slot, gate, hidden, returned):
    routes, f = hidden.shape
    step = 256
    return pl.pallas_call(
        combine_kernel,
        grid=(routes // step,),
        out_shape=(
            jax.ShapeDtypeStruct((routes, f), jnp.bfloat16),
            jax.ShapeDtypeStruct((routes, 1), jnp.float32),
        ),
        in_specs=[
            pl.BlockSpec((step, 1), lambda i: (i, 0)),
            pl.BlockSpec((step, 1), lambda i: (i, 0)),
            pl.BlockSpec((step, f), lambda i: (i, 0)),
            pl.BlockSpec(returned.shape, lambda i: (0, 0)),
        ],
        out_specs=(
            pl.BlockSpec((step, f), lambda i: (i, 0)),
            pl.BlockSpec((step, 1), lambda i: (i, 0)),
        ),
        name="combine",
    )(slot, gate, hidden, returned)


def body(
    out_grad, hidden_saved, gate_probs, expert_ids, weight_q, weight_exp, master, moment1, moment2
):
    f32, bf = jnp.float32, jnp.bfloat16
    tokens, top = expert_ids.shape
    held, rows, width = weight_q.shape
    hid = hidden_saved.shape[2]
    groups = lax.axis_size("expert")
    experts = groups * held
    routes = tokens * top

    gate_col = gate_probs.reshape(routes, 1)
    hidden = hidden_saved.reshape(routes, hid)
    weighted = (gate_probs[..., None] * hidden_saved.astype(f32)).astype(bf).reshape(routes, hid)
    ids = expert_ids.reshape(1, routes)
    sent, code, slot = prep(ids, expert_ids.T, weighted, experts)

    scales = jnp.exp2(weight_exp.astype(f32))
    blocks = weight_exp.shape[2]
    weight = (
        (weight_q.astype(f32).reshape(held, rows, blocks, width // blocks) * scales[..., None])
        .reshape(held, rows, width)
        .astype(bf)
    )
    r_dy, r_w, r_code, w_full = dispatch(
        out_grad,
        sent.reshape(groups, held * CAP, hid),
        code.reshape(groups, held, tokens),
        weight,
    )
    pick = (
        r_code[:, :, None, :] == jnp.arange(CAP, dtype=f32)[None, None, :, None]
    ).astype(bf).reshape(groups, held * CAP, tokens)
    rows_dy = jnp.einsum("sct,std->scd", pick, r_dy, preferred_element_type=f32).astype(bf)
    rows_dy = rows_dy.reshape(groups, held, CAP, width)
    rows_w = r_w.reshape(groups, held, CAP, hid)
    back = jnp.einsum(
        "secd,xefd->secxf", rows_dy, w_full, preferred_element_type=f32
    ).astype(bf)
    grad = jnp.einsum(
        "secxf,secd->xefd",
        rows_w.reshape(groups, held, CAP, NX, rows),
        rows_dy,
        preferred_element_type=f32,
    )
    r_back, r_grad = giveback(back.reshape(groups, held * CAP, hid), grad.astype(bf))
    hidden_grad, gate_grad = combine(
        slot.reshape(routes, 1), gate_col, hidden, r_back.reshape(experts * CAP, hid)
    )

    own = lax.dynamic_index_in_dim(grad, lax.axis_index("fsdp"), 0, keepdims=False)
    summed = own + jnp.sum(r_grad.astype(f32), axis=0)
    summed = summed.reshape(held, 2, rows // 2, width)
    me = lax.axis_index("replica")
    other = lax.dynamic_index_in_dim(summed, 1 - me, 1, keepdims=False)
    got = lax.ppermute(other.astype(bf), "replica", [(0, 1), (1, 0)])
    gradient = lax.dynamic_index_in_dim(summed, me, 1, keepdims=False) + got.astype(f32)

    first = 0.9 * moment1.astype(f32) + 0.1 * gradient
    second = 0.95 * moment2.astype(f32) + 0.05 * gradient * gradient
    update = first / (1.0 - 0.9**20) / (jnp.sqrt(second / (1.0 - 0.95**20)) + 1e-08) + 0.1 * master
    return (
        hidden_grad.reshape(tokens, top, hid),
        gate_grad.reshape(tokens, top),
        master - 0.001 * update,
        first.astype(bf),
        second.astype(bf),
    )


def solution(mesh):
    tok = ("expert", "fsdp", "replica")
    in_specs = (
        P(tok, None),
        P(tok, None, None),
        P(tok, None),
        P(tok, None),
        P("expert", "fsdp", None),
        P("expert", "fsdp", None),
        P("expert", ("fsdp", "replica"), None),
        P("expert", ("fsdp", "replica"), None),
        P("expert", ("fsdp", "replica"), None),
    )
    out_specs = (
        P(tok, None, None),
        P(tok, None),
        P("expert", ("fsdp", "replica"), None),
        P("expert", ("fsdp", "replica"), None),
        P("expert", ("fsdp", "replica"), None),
    )
    return jax.shard_map(body, mesh=mesh, in_specs=in_specs, out_specs=out_specs, check_vma=False)
```

```python
import jax
import jax.numpy as jnp
from jax import lax
from jax.experimental import pallas as pl
from jax.experimental.pallas import tpu as pltpu
from jax.sharding import PartitionSpec as P

MESH = pl.DeviceIdType.MESH
NY, NZ, NZL, NX = 4, 8, 4, 4
CAP = 32
F32, BF = jnp.float32, jnp.bfloat16
ANY = pl.BlockSpec(memory_space=pl.ANY)
VMEM = pl.BlockSpec(memory_space=pltpu.VMEM)


class Place:
    def __init__(self):
        self.own = lax.axis_index("expert")
        self.core = lax.rem(self.own, 2)
        self.y = self.own // (2 * NZL)
        self.half = lax.axis_index("replica")
        self.z = self.half * NZL + lax.rem(self.own // 2, NZL)
        self.x = lax.axis_index("fsdp")
        self.s = 1 - 2 * self.core

    def slot(self, dy, dz, core):
        y = lax.rem(self.y + dy + NY, NY)
        zl = lax.rem(self.z + dz + NZ, NZL)
        return (y * NZL + zl) * 2 + core

    def dev(self, dy, dz, core):
        return {
            "expert": self.slot(dy, dz, core),
            "replica": lax.rem(self.z + dz + NZ, NZ) // NZL,
        }

    def dev_x(self, dx):
        return {"fsdp": lax.rem(self.x + dx + NX, NX)}

    def around(self, i):
        return self.s * ((1 - i % 2) * (i // 2) - (i % 2) * ((i + 1) // 2))


def remote(src, dst, ssem, rsem, dev):
    return pltpu.make_async_remote_copy(
        src_ref=src, dst_ref=dst, send_sem=ssem, recv_sem=rsem, device_id=dev, device_id_type=MESH
    )


def peers(p, far):
    out = []
    for dy in (2, 1, -1, 0):
        for kind in (2, 1, 3, 0):
            for dc in (0, 1):
                core = p.core if dc == 0 else 1 - p.core
                if dc == 0 and dy == 0 and kind == 0:
                    continue
                dz = (0, 1, far(core), -1)[kind]
                out.append((p.dev(dy, dz, core), dy))
    return out


def before(n):
    row = lax.broadcasted_iota(jnp.int32, (n, n), 0)
    return (row < lax.broadcasted_iota(jnp.int32, (n, n), 1)).astype(F32).astype(BF)


def whole_kernel(
    dy_ref, ids_ref, ids_t_ref, hid_ref, gate_ref, ids_c_ref, wq_ref, we_ref,
    hg_ref, gg_ref, gs_ref,
    rdy, rids, rw, ws, wf, xs, wt, own_g, rg, rback, ez_s, ez_r, code, g_tile,
    dy_ss, dy_rs, sib_ss, sib_rs, id_ss, id_rs, b_ss, b_rs, w_ss, w_rs, d_ss, d_rs, e_ss, e_rs,
    z_ss, z_rs, l_sem,
):
    p = Place()
    core, s = p.core, p.s
    tokens, width = dy_ref.shape
    held, rows, _ = wq_ref.shape
    routes, hid = hid_ref.shape
    groups = rids.shape[0]
    half = tokens // 2
    slots = held * CAP
    early, dys = [], []
    count = [0, 0, 0]

    def start(c, to):
        c.start()
        to.append(c)

    def part(slot, h):
        return rdy.at[pl.ds(pl.multiple_of(slot * tokens + h * half, half), half)]

    def block(slot):
        return rdy.at[pl.ds(pl.multiple_of(slot * tokens, tokens), tokens)]

    def at(h, a, b):
        return (a, b) if h == 0 else (b, a)

    def send_dy(src, slot, h, dev):
        k = count[h]
        count[h] += 1
        start(remote(src, part(slot, h), dy_ss.at[h, k], dy_rs.at[h, slot], dev), dys)

    def wait_dy(slot, h):
        blk = part(slot, h)
        remote(blk, blk, dy_ss.at[h, 0], dy_rs.at[h, slot], p.dev(1, 0, core)).wait_recv()

    def send_sib(src, slot):
        k = count[2]
        count[2] += 1
        start(remote(src, block(slot), sib_ss.at[k], sib_rs.at[slot], p.dev(0, 0, 1 - core)), dys)

    def wait_sib(slot):
        blk = block(slot)
        remote(blk, blk, sib_ss.at[0], sib_rs.at[slot], p.dev(0, 0, 1 - core)).wait_recv()

    def mine(h):
        return dy_ref.at[pl.ds(h * half, half)]

    for h in (0, 1):
        for d in (1, -1):
            send_dy(mine(h), p.own, h, p.dev(*at(h, d, 0), core))
    for h in (0, 1):
        for d in (1, -1):
            send_dy(mine(h), p.own, h, p.dev(*at(h, 0, d), core))
    send_sib(dy_ref, p.own)
    there = peers(p, lambda c: 2 * s)
    for k, (dev, _) in enumerate(there):
        start(remote(ids_t_ref, rids.at[p.own], id_ss.at[k], id_rs.at[p.own], dev), early)
    local = [
        pltpu.make_async_copy(dy_ref, block(p.own), l_sem.at[0]),
        pltpu.make_async_copy(ids_t_ref, rids.at[p.own], l_sem.at[1]),
    ]
    for c in local:
        c.start()

    def shard(x):
        return wf.at[:, pl.ds(pl.multiple_of(x * rows, rows), rows)]

    mine_w = pl.ds(pl.multiple_of(p.x * rows, rows), rows)
    qb = width // we_ref.shape[2]
    for e in range(held):
        scale = jnp.exp2(we_ref[e].astype(F32))
        for j in range(we_ref.shape[2]):
            cols = pl.ds(j * qb, qb)
            wf[e, mine_w, cols] = (wq_ref[e, :, cols].astype(F32) * scale[:, j : j + 1]).astype(BF)

    experts = groups * held
    ids = ids_ref[...]
    named = jnp.where(
        ids == lax.broadcasted_iota(jnp.int32, (experts, routes), 0), 1.0, 0.0
    ).astype(F32)
    rank = jnp.dot(named.astype(BF), before(routes), preferred_element_type=F32)
    slot_row = ids * CAP + jnp.sum(named * rank, axis=0, keepdims=True).astype(jnp.int32)
    hg_ref[...] = (gate_ref[...] * hid_ref[...].astype(F32)).astype(BF)

    for i, dx in enumerate((1, -1)):
        start(remote(shard(p.x), shard(p.x), w_ss.at[i], w_rs.at[p.x], p.dev_x(dx)), early)

    step = 256
    per = step // slots

    def fill(i, _):
        lo = i * step
        pick = (slot_row == lax.broadcasted_iota(jnp.int32, (step, routes), 0) + lo).astype(F32)
        got = jnp.dot(pick.astype(BF), hg_ref[...], preferred_element_type=F32).astype(BF)
        ws[pl.ds(i * per, per)] = got.reshape(per, slots, hid)
        return 0

    lax.fori_loop(0, groups // per, fill, 0)

    for h in (0, 1):
        b = p.slot(*at(h, -s, 0), core)
        wait_dy(b, h)
        send_dy(part(b, h), b, h, p.dev(*at(h, s, 0), core))
        for d in (1, -1):
            send_dy(part(b, h), b, h, p.dev(*at(h, 0, d), core))

    def send_rows(lo, hi):
        for k in range(lo, hi):
            dev = there[k][0]
            start(remote(ws.at[dev["expert"]], rw.at[p.own], b_ss.at[k], b_rs.at[p.own], dev), early)

    own_rows = pltpu.make_async_copy(ws.at[p.own], rw.at[p.own], l_sem.at[2])
    own_rows.start()
    send_rows(0, 8)
    for a in (s, -2 * s):
        for h in (0, 1):
            b = p.slot(*at(h, a, 0), core)
            wait_dy(b, h)
            for d in (1, -1):
                send_dy(part(b, h), b, h, p.dev(*at(h, 0, d), core))
    send_rows(8, 16)
    for a in (0, -s, s, -2 * s):
        for h in (0, 1):
            b = p.slot(*at(h, a, -s), core)
            wait_dy(b, h)
            send_dy(part(b, h), b, h, p.dev(*at(h, 0, s), core))
    send_rows(16, 31)

    back_x = lax.rem(p.x - s + NX, NX)
    remote(shard(back_x), shard(back_x), w_ss.at[2], w_rs.at[back_x], p.dev_x(s)).wait_recv()
    start(remote(shard(back_x), shard(back_x), w_ss.at[2], w_rs.at[back_x], p.dev_x(s)), early)

    local[1].wait()
    for dc in (0, 1):
        c2 = core if dc == 0 else 1 - core
        for dy in range(NY):
            for dz in range(NZL):
                if dc == 0 and dy == 0 and dz == 0:
                    continue
                j = p.slot(dy, dz, c2)
                remote(
                    rids.at[j], rids.at[j], id_ss.at[0], id_rs.at[j], p.dev(1, 0, core)
                ).wait_recv()
    tri = before(tokens)
    for e in range(held):
        hit = jnp.sum((rids[...] == p.own * held + e).astype(F32), axis=1)
        code[e] = jnp.where(
            hit > 0, jnp.dot(hit.astype(BF), tri, preferred_element_type=F32), -1.0
        )

    def pick_rows(j):
        lane = lax.broadcasted_iota(jnp.int32, (CAP, tokens), 0).astype(F32)
        pick = jnp.concatenate(
            [(code[e, pl.ds(j, 1), :] == lane).astype(F32) for e in range(held)], axis=0
        ).astype(BF)
        got = jnp.dot(pick, block(j)[...], preferred_element_type=F32).astype(BF)
        for e in range(held):
            xs[e, pl.ds(pl.multiple_of(j * CAP, CAP), CAP)] = got[e * CAP : (e + 1) * CAP]

    def pair(g, k):
        t = g // (k + 1)
        return (1 - t) * g + t * k, (1 - t) * k + t * (g - k - 1)

    def own_stage(k):
        offs = (0, -s, s, -2 * s)
        pairs = [(i, k) for i in range(k)] + [(k, j) for j in range(k)] + [(k, k)]
        for i, j in pairs:
            b = p.slot(offs[i], offs[j], core)
            if j > 1:
                wait_dy(b, 0)
            if i > 1:
                wait_dy(b, 1)
            send_sib(block(b), b)

        def one(g, _):
            i, j = pair(g, k)
            pick_rows(p.slot(p.around(i), p.around(j), core))
            return 0

        lax.fori_loop(0, 2 * k + 1, one, 0)

    def sib_stage(k):
        def one(g, _):
            i, j = pair(g, k)
            b = p.slot(-p.around(i), -p.around(j), 1 - core)
            wait_sib(b)
            pick_rows(b)
            return 0

        lax.fori_loop(0, 2 * k + 1, one, 0)

    local[0].wait()
    pick_rows(p.own)
    own_stage(1)
    sib_stage(0)
    own_stage(2)
    sib_stage(1)
    own_stage(3)
    sib_stage(2)
    sib_stage(3)

    own_rows.wait()
    for dc in (0, 1):
        c2 = core if dc == 0 else 1 - core
        for dy in range(NY):
            for dz in range(NZL):
                if dc == 0 and dy == 0 and dz == 0:
                    continue
                j = p.slot(dy, dz, c2)
                remote(rw.at[j], rw.at[j], b_ss.at[0], b_rs.at[j], p.dev(1, 0, core)).wait_recv()
    for c in dys:
        c.wait_send()

    chunk = groups * CAP // 4
    for e in range(held):
        for i in range(4):
            got = rw[i * 8 : (i + 1) * 8, e * CAP : (e + 1) * CAP].reshape(chunk, hid)
            wt[e, :, i * chunk : (i + 1) * chunk] = got.T
    piece = width // 2
    nt = 256
    own_at = pl.ds(pl.multiple_of(p.x * rows, rows), rows)
    late = []
    for e in range(held):
        for h in (0, 1):

            def tile(n, _):
                cols = pl.ds(pl.multiple_of(h * piece + n * nt, nt), nt)
                g = jnp.dot(wt[e], xs[e, :, cols], preferred_element_type=F32)
                rdy[e * hid : (e + 1) * hid, cols] = g.astype(BF)
                g_tile[...] = g
                own_g[e, :, cols] = g_tile[own_at]
                return 0

            lax.fori_loop(0, piece // nt, tile, 0)
            cols = pl.ds(h * piece, piece)
            for k, dx in enumerate((1, -1, 2)):
                to = lax.rem(p.x + dx + NX, NX)
                src = rdy.at[pl.ds(pl.multiple_of(e * hid + to * rows, rows), rows), cols]
                start(
                    remote(
                        src, rg.at[k, e, :, cols], e_ss.at[e, h, k], e_rs.at[e, h, k], p.dev_x(dx)
                    ),
                    late,
                )

    for dx in (1, 2):
        j = lax.rem(p.x + dx * s + 2 * NX, NX)
        remote(shard(j), shard(j), w_ss.at[0], w_rs.at[j], p.dev_x(1)).wait_recv()
    for c in early:
        c.wait_send()
    home = peers(p, lambda c: 4 * c - 2)
    k = 0
    for dy in (2, 1, -1, 0):
        yy = lax.rem(p.y + dy + NY, NY)
        for e in range(held):
            x_rows = xs[e, pl.ds(pl.multiple_of(yy * 256, 256), 256)]
            got = lax.dot_general(
                x_rows, wf[e], (((1,), (1,)), ((), ())), preferred_element_type=F32
            )
            ws[pl.ds(yy * 8, 8), e * CAP : (e + 1) * CAP] = got.astype(BF).reshape(8, CAP, hid)
        for dev, dy2 in home:
            if dy2 == dy:
                start(
                    remote(
                        ws.at[dev["expert"]], rback.at[p.own], d_ss.at[k], d_rs.at[p.own], dev
                    ),
                    late,
                )
                k += 1
    own_back = pltpu.make_async_copy(ws.at[p.own], rback.at[p.own], l_sem.at[3])
    own_back.start()

    keep = rows // 2

    def reduce_piece(e, h):
        cols = pl.ds(h * piece, piece)
        for k in range(3):
            a = rg.at[k, e, :, cols]
            remote(a, a, e_ss.at[e, h, k], e_rs.at[e, h, k], p.dev_x(1)).wait_recv()

        def total(r):
            at_r = pl.ds(pl.multiple_of(r * keep, keep), keep)
            t = own_g[e, at_r, cols]
            for k in range(3):
                t += rg[k, e, at_r, cols].astype(F32)
            return t

        ez_s[e, :, cols] = total(1 - p.half).astype(BF)
        gs_ref[e, :, cols] = total(p.half)
        start(
            remote(
                ez_s.at[e, :, cols], ez_r.at[e, :, cols], z_ss.at[e, h], z_rs.at[e, h],
                {"replica": 1 - p.half},
            ),
            late,
        )

    reduce_piece(0, 0)
    reduce_piece(0, 1)

    own_back.wait()
    for dc in (0, 1):
        c2 = core if dc == 0 else 1 - core
        for dy in range(NY):
            for dz in range(NZL):
                if dc == 0 and dy == 0 and dz == 0:
                    continue
                j = p.slot(dy, dz, c2)
                remote(
                    rback.at[j], rback.at[j], d_ss.at[0], d_rs.at[j], p.dev(1, 0, core)
                ).wait_recv()

    named_c = ids_c_ref[...] == lax.broadcasted_iota(jnp.int32, (routes, experts), 1)
    named_c = jnp.where(named_c, 1.0, 0.0).astype(BF)

    def join(i, _):
        r = pl.ds(pl.multiple_of(i * step, step), step)
        here = lax.broadcasted_iota(jnp.int32, (step, routes), 0) + i * step
        older = (lax.broadcasted_iota(jnp.int32, (step, routes), 1) < here).astype(F32)
        rank = jnp.dot(older.astype(BF), named_c, preferred_element_type=F32)
        mine = ids_c_ref[r] == lax.broadcasted_iota(jnp.int32, (step, experts), 1)
        rank = jnp.sum(jnp.where(mine, rank, 0.0), axis=1, keepdims=True)
        slot_c = ids_c_ref[r] * CAP + rank.astype(jnp.int32)
        pick = slot_c == lax.broadcasted_iota(jnp.int32, (step, groups * slots), 1)
        got = jnp.dot(
            pick.astype(F32).astype(BF),
            rback[...].reshape(groups * slots, hid),
            preferred_element_type=F32,
        )
        hg_ref[r] = (gate_ref[r] * got).astype(BF)
        gg_ref[r] = jnp.sum(hid_ref[r].astype(F32) * got, axis=1, keepdims=True)
        return 0

    lax.fori_loop(0, routes // step, join, 0)

    reduce_piece(1, 0)
    reduce_piece(1, 1)
    for e in range(held):
        for h in (0, 1):
            cols = pl.ds(h * piece, piece)
            a = ez_r.at[e, :, cols]
            remote(a, a, z_ss.at[e, h], z_rs.at[e, h], p.dev_x(1)).wait_recv()
            gs_ref[e, :, cols] += ez_r[e, :, cols].astype(F32)
    for c in late:
        c.wait_send()


def whole(dy, ids, ids_t, hidden, gate, ids_c, wq, we):
    tokens, width = dy.shape
    held, rows, _ = wq.shape
    routes, hid = hidden.shape
    groups = lax.axis_size("expert")
    slots = held * CAP
    full = rows * NX
    dma = pltpu.SemaphoreType.DMA
    vm = pltpu.VMEM
    return pl.pallas_call(
        whole_kernel,
        out_shape=(
            jax.ShapeDtypeStruct((routes, hid), BF),
            jax.ShapeDtypeStruct((routes, 1), F32),
            jax.ShapeDtypeStruct((held, rows // 2, width), F32),
        ),
        in_specs=[VMEM] * 8,
        out_specs=(VMEM,) * 3,
        scratch_shapes=[
            vm((groups * tokens, width), BF),
            vm((groups,) + ids_t.shape, jnp.int32),
            vm((groups, slots, hid), BF),
            vm((groups, slots, hid), BF),
            vm((held, full, width), BF),
            vm((held, groups * CAP, width), BF),
            vm((held, hid, groups * CAP), BF),
            vm((held, rows, width), F32),
            vm((NX - 1, held, rows, width), BF),
            vm((groups, slots, hid), BF),
            vm((held, rows // 2, width), BF),
            vm((held, rows // 2, width), BF),
            vm((held, groups, tokens), F32),
            vm((hid, 256), F32),
            dma((2, 15)), dma((2, 32)), dma((16,)), dma((32,)), dma((31,)), dma((32,)),
            dma((31,)), dma((32,)), dma((3,)), dma((4,)), dma((31,)), dma((32,)),
            dma((2, 2, 3)), dma((2, 2, 3)), dma((2, 2)), dma((2, 2)), dma((4,)),
        ],
        compiler_params=pltpu.CompilerParams(
            has_side_effects=True, vmem_limit_bytes=67043328
        ),
        name="whole",
    )(dy, ids, ids_t, hidden, gate, ids_c, wq, we)


def body(
    out_grad, hidden_saved, gate_probs, expert_ids, weight_q, weight_exp, master, moment1, moment2
):
    tokens, top = expert_ids.shape
    hid = hidden_saved.shape[2]
    routes = tokens * top

    ids = expert_ids.reshape(1, routes)
    hidden_grad, gate_grad, gradient = whole(
        out_grad,
        ids,
        expert_ids.T,
        hidden_saved.reshape(routes, hid),
        gate_probs.reshape(routes, 1),
        expert_ids.reshape(routes, 1),
        weight_q,
        weight_exp,
    )
    first = 0.9 * moment1.astype(F32) + 0.1 * gradient
    second = 0.95 * moment2.astype(F32) + 0.05 * gradient * gradient
    update = first / (1.0 - 0.9**20) / (jnp.sqrt(second / (1.0 - 0.95**20)) + 1e-08) + 0.1 * master
    return (
        hidden_grad.reshape(tokens, top, hid),
        gate_grad.reshape(tokens, top),
        master - 0.001 * update,
        first.astype(BF),
        second.astype(BF),
    )


def solution(mesh):
    tok = ("expert", "fsdp", "replica")
    in_specs = (
        P(tok, None),
        P(tok, None, None),
        P(tok, None),
        P(tok, None),
        P("expert", "fsdp", None),
        P("expert", "fsdp", None),
        P("expert", ("fsdp", "replica"), None),
        P("expert", ("fsdp", "replica"), None),
        P("expert", ("fsdp", "replica"), None),
    )
    out_specs = (
        P(tok, None, None),
        P(tok, None),
        P("expert", ("fsdp", "replica"), None),
        P("expert", ("fsdp", "replica"), None),
        P("expert", ("fsdp", "replica"), None),
    )
    return jax.shard_map(body, mesh=mesh, in_specs=in_specs, out_specs=out_specs, check_vma=False)
```

```python
import jax
import jax.numpy as jnp
from jax import lax
from jax.experimental import pallas as pl
from jax.experimental.pallas import tpu as pltpu
from jax.sharding import PartitionSpec as P

MESH = pl.DeviceIdType.MESH
NY, NZ, NZL, NX = 4, 8, 4, 4
CAP = 32
F32, BF = jnp.float32, jnp.bfloat16
ANY = pl.BlockSpec(memory_space=pl.ANY)
VMEM = pl.BlockSpec(memory_space=pltpu.VMEM)


class Place:
    def __init__(self):
        self.own = lax.axis_index("expert")
        self.core = lax.rem(self.own, 2)
        self.y = self.own // (2 * NZL)
        self.half = lax.axis_index("replica")
        self.z = self.half * NZL + lax.rem(self.own // 2, NZL)
        self.x = lax.axis_index("fsdp")
        self.s = 1 - 2 * self.core

    def slot(self, dy, dz, core):
        y = lax.rem(self.y + dy + NY, NY)
        zl = lax.rem(self.z + dz + NZ, NZL)
        return (y * NZL + zl) * 2 + core

    def dev(self, dy, dz, core):
        return {
            "expert": self.slot(dy, dz, core),
            "replica": lax.rem(self.z + dz + NZ, NZ) // NZL,
        }

    def dev_x(self, dx):
        return {"fsdp": lax.rem(self.x + dx + NX, NX)}

    def around(self, i):
        return self.s * ((1 - i % 2) * (i // 2) - (i % 2) * ((i + 1) // 2))


def remote(src, dst, ssem, rsem, dev):
    return pltpu.make_async_remote_copy(
        src_ref=src, dst_ref=dst, send_sem=ssem, recv_sem=rsem, device_id=dev, device_id_type=MESH
    )


def peers(p, far):
    out = []
    for dy in (1, -1, 0):
        for kind in (2, 1, 3, 0):
            for dc in (0, 1):
                core = p.core if dc == 0 else 1 - p.core
                if dc == 0 and dy == 0 and kind == 0:
                    continue
                dz = (0, 1, far(core), -1)[kind]
                out.append((p.dev(dy, dz, core), dy))
    return out


def far_row(p, dy, far):
    return [
        p.dev(dy, (0, 1, far(c), -1)[kind], c)
        for kind in range(NZL)
        for c in (p.core, 1 - p.core)
    ]


def spread(rows):
    k, t = rows.shape
    wide = jnp.broadcast_to(rows[None], (t, k, t)).reshape(t * k, t)
    at_t = lax.broadcasted_iota(jnp.int32, (t * k, t), 0) // k
    here = at_t == lax.broadcasted_iota(jnp.int32, (t * k, t), 1)
    return jnp.sum(jnp.where(here, wide, jnp.zeros_like(wide)), axis=1, keepdims=True)


def before(n):
    row = lax.broadcasted_iota(jnp.int32, (n, n), 0)
    return (row < lax.broadcasted_iota(jnp.int32, (n, n), 1)).astype(F32).astype(BF)


def whole_kernel(
    dy_ref, ids_t_ref, hid_ref, gate_ref, wq_ref, we_ref,
    hg_ref, gg_ref, gs_ref,
    rdy, rids, rw, ws, wf, xs, wt, own_g, rg, rback, b_via, d_via, ez_s, ez_t, ez_r, code, g_tile,
    dy_ss, dy_rs, sib_ss, sib_rs, id_ss, id_rs, b_ss, b_rs, w_ss, w_rs, d_ss, d_rs, e_ss, e_rs,
    v_rs, z_ss, z_rs, l_sem,
):
    p = Place()
    core, s = p.core, p.s
    tokens, width = dy_ref.shape
    held, rows, _ = wq_ref.shape
    routes, hid = hid_ref.shape
    groups = rids.shape[0]
    half = tokens // 2
    slots = held * CAP
    early, dys = [], []
    count = [0, 0, 0]

    def start(c, to):
        c.start()
        to.append(c)

    def part(slot, h):
        return rdy.at[pl.ds(pl.multiple_of(slot * tokens + h * half, half), half)]

    def block(slot):
        return rdy.at[pl.ds(pl.multiple_of(slot * tokens, tokens), tokens)]

    def at(h, a, b):
        return (a, b) if h == 0 else (b, a)

    def send_dy(src, slot, h, dev):
        k = count[h]
        count[h] += 1
        start(remote(src, part(slot, h), dy_ss.at[h, k], dy_rs.at[h, slot], dev), dys)

    def wait_dy(slot, h):
        blk = part(slot, h)
        remote(blk, blk, dy_ss.at[h, 0], dy_rs.at[h, slot], p.dev(1, 0, core)).wait_recv()

    def send_sib(src, slot):
        k = count[2]
        count[2] += 1
        start(remote(src, block(slot), sib_ss.at[k], sib_rs.at[slot], p.dev(0, 0, 1 - core)), dys)

    def wait_sib(slot):
        blk = block(slot)
        remote(blk, blk, sib_ss.at[0], sib_rs.at[slot], p.dev(0, 0, 1 - core)).wait_recv()

    gate = pltpu.get_barrier_semaphore()
    near = [dev for dev, _ in peers(p, lambda c: 2 * s)] + far_row(p, 2, lambda c: 2 * s)
    near += [p.dev(dy, -2 * s, core) for dy in range(NY)]
    near += [p.dev_x(d) for d in (1, 2, 3)] + [{"replica": 1 - p.half}]
    for dev in near:
        pl.semaphore_signal(gate, inc=1, device_id=dev, device_id_type=MESH)
    pl.semaphore_wait(gate, len(near))

    def mine(h):
        return dy_ref.at[pl.ds(h * half, half)]

    for h in (0, 1):
        for d in (1, -1):
            send_dy(mine(h), p.own, h, p.dev(*at(h, d, 0), core))
    for h in (0, 1):
        for d in (1, -1):
            send_dy(mine(h), p.own, h, p.dev(*at(h, 0, d), core))
    send_sib(dy_ref, p.own)
    there = peers(p, lambda c: 2 * s)
    for k, dev in enumerate([dev for dev, _ in there] + far_row(p, 2, lambda c: 2 * s)):
        start(remote(ids_t_ref, rids.at[p.own], id_ss.at[k], id_rs.at[p.own], dev), early)
    local = [
        pltpu.make_async_copy(dy_ref, block(p.own), l_sem.at[0]),
        pltpu.make_async_copy(ids_t_ref, rids.at[p.own], l_sem.at[1]),
    ]
    for c in local:
        c.start()

    def shard(x):
        return wf.at[:, pl.ds(pl.multiple_of(x * rows, rows), rows)]

    mine_w = pl.ds(pl.multiple_of(p.x * rows, rows), rows)
    qb = width // we_ref.shape[1]
    for e in range(held):
        blocks = we_ref.shape[1]
        same = lax.broadcasted_iota(jnp.int32, (blocks, blocks), 0) == lax.broadcasted_iota(
            jnp.int32, (blocks, blocks), 1
        )
        power = lax.dot_general(
            we_ref[e].astype(F32).astype(BF), same.astype(F32).astype(BF),
            (((0,), (0,)), ((), ())), preferred_element_type=F32,
        )
        scale = jnp.exp2(power)
        for j in range(blocks):
            cols = pl.ds(j * qb, qb)
            wf[e, mine_w, cols] = (wq_ref[e, :, cols].astype(F32) * scale[:, j : j + 1]).astype(BF)

    experts = groups * held
    ids_t = ids_t_ref[...]
    top = ids_t.shape[0]
    expert = lax.broadcasted_iota(jnp.int32, (experts, tokens), 0)
    named = jnp.zeros((experts, tokens), F32)
    for k in range(top):
        named += (ids_t[k : k + 1] == expert).astype(F32)
    rank = jnp.dot(named.astype(BF), before(tokens), preferred_element_type=F32)
    rank_t = jnp.concatenate(
        [
            jnp.sum(jnp.where(ids_t[k : k + 1] == expert, rank, 0.0), axis=0, keepdims=True)
            for k in range(top)
        ],
        axis=0,
    )
    slot_t = ids_t * CAP + rank_t.astype(jnp.int32)
    both = jnp.concatenate([ids_t.astype(F32), rank_t], axis=0).astype(BF)
    lane_t = lax.broadcasted_iota(jnp.int32, (tokens, routes), 1) // top
    over = (lane_t == lax.broadcasted_iota(jnp.int32, (tokens, routes), 0)).astype(F32)
    both = jnp.dot(both, over.astype(BF), preferred_element_type=F32)
    mine_k = lax.rem(
        lax.broadcasted_iota(jnp.int32, (top, routes), 1), top
    ) == lax.broadcasted_iota(jnp.int32, (top, routes), 0)
    slot_row = jnp.sum(
        jnp.where(mine_k, both[:top] * CAP + both[top:], 0.0), axis=0, keepdims=True
    ).astype(jnp.int32)
    hg_ref[...] = (spread(gate_ref[...]) * hid_ref[...].astype(F32)).astype(BF)

    for i, dx in enumerate((1, -1)):
        start(remote(shard(p.x), shard(p.x), w_ss.at[i], w_rs.at[p.x], p.dev_x(dx)), early)

    step = 256
    per = step // slots

    def fill(i, _):
        lo = i * step
        pick = (slot_row == lax.broadcasted_iota(jnp.int32, (step, routes), 0) + lo).astype(F32)
        got = jnp.dot(pick.astype(BF), hg_ref[...], preferred_element_type=F32).astype(BF)
        ws[pl.ds(i * per, per)] = got.reshape(per, slots, hid)
        return 0

    lax.fori_loop(0, groups // per, fill, 0)

    for h in (0, 1):
        b = p.slot(*at(h, -s, 0), core)
        wait_dy(b, h)
        send_dy(part(b, h), b, h, p.dev(*at(h, s, 0), core))
        for d in (1, -1):
            send_dy(part(b, h), b, h, p.dev(*at(h, 0, d), core))

    def of_expert(ref, j, e):
        return ref.at[j, pl.ds(e * CAP, CAP)]

    row_sends = [[] for _ in range(held)]

    def far_rows(ref, e, y):
        y = lax.rem(y + 2 * NY, NY)
        return ref.at[pl.ds(y * 2 * NZL, 2 * NZL), pl.ds(e * CAP, CAP)]

    def send_rows(e):
        far = far_rows(ws, e, p.y + 2)
        via = b_via.at[:, pl.ds(e * CAP, CAP)]
        start(remote(far, via, b_ss.at[e, 31], v_rs.at[0, e], p.dev(s, 0, core)), row_sends[e])
        for k in range(23):
            dev = there[k][0]
            src, dst = of_expert(ws, dev["expert"], e), of_expert(rw, p.own, e)
            start(remote(src, dst, b_ss.at[e, k], b_rs.at[e, p.own], dev), row_sends[e])

    def pass_rows(via, dst, e, k, ss, rs, far, to):
        blk = via.at[:, pl.ds(e * CAP, CAP)]
        remote(blk, blk, ss.at[e, 31], v_rs.at[k, e], p.dev(s, 0, core)).wait_recv()
        origin = p.slot(-s, 0, core)
        for i, dev in enumerate(far_row(p, s, far)):
            src = of_expert(via, lax.rem(dev["expert"], 2 * NZL), e)
            start(
                remote(src, of_expert(dst, origin, e), ss.at[e, 23 + i], rs.at[e, origin], dev), to
            )

    own_rows = pltpu.make_async_copy(ws.at[p.own], rw.at[p.own], l_sem.at[2])
    own_rows.start()
    send_rows(0)
    for a in (s, -2 * s):
        for h in (0, 1):
            b = p.slot(*at(h, a, 0), core)
            wait_dy(b, h)
            for d in (1, -1):
                send_dy(part(b, h), b, h, p.dev(*at(h, 0, d), core))
    pass_rows(b_via, rw, 0, 0, b_ss, b_rs, lambda c: 2 * s, row_sends[0])
    for a in (0, -s, s, -2 * s):
        for h in (0, 1):
            b = p.slot(*at(h, a, -s), core)
            wait_dy(b, h)
            send_dy(part(b, h), b, h, p.dev(*at(h, 0, s), core))
    send_rows(1)
    pass_rows(b_via, rw, 1, 0, b_ss, b_rs, lambda c: 2 * s, row_sends[1])

    back_x = lax.rem(p.x - s + NX, NX)
    remote(shard(back_x), shard(back_x), w_ss.at[2], w_rs.at[back_x], p.dev_x(s)).wait_recv()
    start(remote(shard(back_x), shard(back_x), w_ss.at[2], w_rs.at[back_x], p.dev_x(s)), early)

    local[1].wait()
    for dc in (0, 1):
        c2 = core if dc == 0 else 1 - core
        for dy in range(NY):
            for dz in range(NZL):
                if dc == 0 and dy == 0 and dz == 0:
                    continue
                j = p.slot(dy, dz, c2)
                remote(
                    rids.at[j], rids.at[j], id_ss.at[0], id_rs.at[j], p.dev(1, 0, core)
                ).wait_recv()
    tri = before(tokens)
    for e in range(held):
        hit = jnp.sum((rids[...] == p.own * held + e).astype(F32), axis=1)
        code[e] = jnp.where(
            hit > 0, jnp.dot(hit.astype(BF), tri, preferred_element_type=F32), -1.0
        )

    def pick_rows(j):
        lane = lax.broadcasted_iota(jnp.int32, (CAP, tokens), 0).astype(F32)
        pick = jnp.concatenate(
            [(code[e, pl.ds(j, 1), :] == lane).astype(F32) for e in range(held)], axis=0
        ).astype(BF)
        got = jnp.dot(pick, block(j)[...], preferred_element_type=F32).astype(BF)
        for e in range(held):
            xs[e, pl.ds(pl.multiple_of(j * CAP, CAP), CAP)] = got[e * CAP : (e + 1) * CAP]

    def pair(g, k):
        t = g // (k + 1)
        return (1 - t) * g + t * k, (1 - t) * k + t * (g - k - 1)

    def own_stage(k):
        offs = (0, -s, s, -2 * s)
        pairs = [(i, k) for i in range(k)] + [(k, j) for j in range(k)] + [(k, k)]
        for i, j in pairs:
            b = p.slot(offs[i], offs[j], core)
            if j > 1:
                wait_dy(b, 0)
            if i > 1:
                wait_dy(b, 1)
            send_sib(block(b), b)

        def one(g, _):
            i, j = pair(g, k)
            pick_rows(p.slot(p.around(i), p.around(j), core))
            return 0

        lax.fori_loop(0, 2 * k + 1, one, 0)

    def sib_stage(k):
        def one(g, _):
            i, j = pair(g, k)
            b = p.slot(-p.around(i), -p.around(j), 1 - core)
            wait_sib(b)
            pick_rows(b)
            return 0

        lax.fori_loop(0, 2 * k + 1, one, 0)

    local[0].wait()
    pick_rows(p.own)
    own_stage(1)
    sib_stage(0)
    own_stage(2)
    sib_stage(1)
    own_stage(3)
    sib_stage(2)
    sib_stage(3)

    for c in dys:
        c.wait_send()
    own_rows.wait()

    def others():
        for dc in (0, 1):
            c2 = core if dc == 0 else 1 - core
            for dy in range(NY):
                for dz in range(NZL):
                    if dc or dy or dz:
                        yield p.slot(dy, dz, c2)

    chunk = groups * CAP // 4
    piece = width // 2
    nt = 256
    late = []

    def rows_of(e, x):
        x = lax.rem(x + 2 * NX, NX)
        return pl.ds(pl.multiple_of(e * hid + x * rows, rows), rows)

    def weighted_here(e):
        for j in others():
            a = of_expert(rw, j, e)
            remote(a, a, b_ss.at[e, 0], b_rs.at[e, j], p.dev(1, 0, core)).wait_recv()
        for c in row_sends[e]:
            c.wait_send()
        for i in range(4):
            got = rw[i * 8 : (i + 1) * 8, e * CAP : (e + 1) * CAP].reshape(chunk, hid)
            wt[e, :, i * chunk : (i + 1) * chunk] = got.T

    def to_x(e, h, k, x, dx):
        cols = pl.ds(h * piece, piece)
        src = rdy.at[rows_of(e, x), cols]
        dst = rg.at[k, e, :, cols]
        start(remote(src, dst, e_ss.at[e, h, k], e_rs.at[e, h, k], p.dev_x(dx)), late)

    def from_x(e, h, k):
        a = rg.at[k, e, :, pl.ds(h * piece, piece)]
        remote(a, a, e_ss.at[e, h, k], e_rs.at[e, h, k], p.dev_x(1)).wait_recv()

    def grad_piece(e, h):
        def tile(n, _):
            cols = pl.ds(pl.multiple_of(h * piece + n * nt, nt), nt)
            g = jnp.dot(wt[e], xs[e, :, cols], preferred_element_type=F32)
            rdy[e * hid : (e + 1) * hid, cols] = g.astype(BF)
            g_tile[...] = g
            own_g[e, :, cols] = g_tile[mine_w]
            return 0

        lax.fori_loop(0, piece // nt, tile, 0)
        to_x(e, h, 0, p.x + 2 * s, s)
        to_x(e, h, 1, p.x - s, -s)

    def relay_piece(e, h):
        cols = pl.ds(h * piece, piece)
        from_x(e, h, 0)
        r = rows_of(e, p.x + s)
        rdy[r, cols] = (rdy[r, cols].astype(F32) + rg[0, e, :, cols].astype(F32)).astype(BF)
        to_x(e, h, 2, p.x + s, s)

    def back_tile(e, dy):
        yy = lax.rem(p.y + dy + NY, NY)
        x_rows = xs[e, pl.ds(pl.multiple_of(yy * 256, 256), 256)]
        got = lax.dot_general(x_rows, wf[e], (((1,), (1,)), ((), ())), preferred_element_type=F32)
        ws[pl.ds(yy * 8, 8), e * CAP : (e + 1) * CAP] = got.astype(BF).reshape(8, CAP, hid)

    home = peers(p, lambda c: 4 * c - 2)

    def back_rows(e):
        for dy in (2, 1, -1, 0):
            back_tile(e, dy)
            if dy == 2:
                far = far_rows(ws, e, p.y + 2)
                via = d_via.at[:, pl.ds(e * CAP, CAP)]
                c = remote(far, via, d_ss.at[e, 31], v_rs.at[1, e], p.dev(s, 0, core))
                start(c, late)
            for k, (dev, dy2) in enumerate(home):
                if dy2 == dy:
                    src, dst = of_expert(ws, dev["expert"], e), of_expert(rback, p.own, e)
                    start(remote(src, dst, d_ss.at[e, k], d_rs.at[e, p.own], dev), late)

    def pass_back(e):
        pass_rows(d_via, rback, e, 1, d_ss, d_rs, lambda c: 4 * c - 2, late)

    weighted_here(0)
    grad_piece(0, 0)
    for dx in (1, 2):
        j = lax.rem(p.x + dx * s + 2 * NX, NX)
        remote(shard(j), shard(j), w_ss.at[0], w_rs.at[j], p.dev_x(1)).wait_recv()
    back_rows(0)
    relay_piece(0, 0)
    grad_piece(0, 1)
    pass_back(0)
    weighted_here(1)
    relay_piece(0, 1)
    grad_piece(1, 0)
    back_rows(1)
    own_back = pltpu.make_async_copy(ws.at[p.own], rback.at[p.own], l_sem.at[3])
    own_back.start()
    relay_piece(1, 0)
    grad_piece(1, 1)
    pass_back(1)
    for c in early:
        c.wait_send()

    keep = rows // 2

    def to_z(src, dst, k, e, h):
        cols = pl.ds(h * piece, piece)
        c = remote(
            src.at[e, :, cols], dst.at[e, :, cols], z_ss.at[k, e, h], z_rs.at[k, e, h],
            p.dev(0, 2 * s, core),
        )
        start(c, late)

    def from_z(dst, k, e, h):
        a = dst.at[e, :, pl.ds(h * piece, piece)]
        remote(a, a, z_ss.at[k, e, h], z_rs.at[k, e, h], p.dev(0, 2 * s, core)).wait_recv()

    def pass_z(e, h):
        from_z(ez_t, 0, e, h)
        to_z(ez_t, ez_r, 1, e, h)

    def reduce_piece(e, h):
        cols = pl.ds(h * piece, piece)
        from_x(e, h, 1)
        from_x(e, h, 2)

        def total(r):
            at_r = pl.ds(pl.multiple_of(r * keep, keep), keep)
            t = own_g[e, at_r, cols]
            for k in (1, 2):
                t += rg[k, e, at_r, cols].astype(F32)
            return t

        ez_s[e, :, cols] = total(1 - p.half).astype(BF)
        gs_ref[e, :, cols] = total(p.half)
        to_z(ez_s, ez_t, 0, e, h)

    reduce_piece(0, 0)
    relay_piece(1, 1)
    reduce_piece(0, 1)
    pass_z(0, 0)
    reduce_piece(1, 0)
    pass_z(0, 1)

    own_back.wait()
    for j in others():
        for e in range(held):
            a = of_expert(rback, j, e)
            remote(a, a, d_ss.at[e, 0], d_rs.at[e, j], p.dev(1, 0, core)).wait_recv()

    tk = step // top
    sub = lax.broadcasted_iota(jnp.int32, (step, tokens), 0) // top
    lane = lax.broadcasted_iota(jnp.int32, (step, tokens), 1)

    def join(i, _):
        r = pl.ds(pl.multiple_of(i * step, step), step)
        here = sub + i * tk == lane

        def column(rows):
            wide = jnp.broadcast_to(rows[None], (tk, top, tokens)).reshape(step, tokens)
            return jnp.sum(jnp.where(here, wide, jnp.zeros_like(wide)), axis=1, keepdims=True)

        pick = column(slot_t) == lax.broadcasted_iota(jnp.int32, (step, groups * slots), 1)
        got = jnp.dot(
            pick.astype(F32).astype(BF),
            rback[...].reshape(groups * slots, hid),
            preferred_element_type=F32,
        )
        hg_ref[r] = (column(gate_ref[...]) * got).astype(BF)
        dots = jnp.sum(hid_ref[r].astype(F32) * got, axis=1, keepdims=True)
        gg_ref[...] += jnp.sum(
            jnp.where(here, dots, 0.0).reshape(tk, top, tokens), axis=0
        )
        return 0

    gg_ref[...] = jnp.zeros_like(gg_ref)
    lax.fori_loop(0, routes // step, join, 0)

    pass_z(1, 0)
    reduce_piece(1, 1)
    pass_z(1, 1)
    for e in range(held):
        for h in (0, 1):
            cols = pl.ds(h * piece, piece)
            from_z(ez_r, 1, e, h)
            gs_ref[e, :, cols] += ez_r[e, :, cols].astype(F32)
    for c in late:
        c.wait_send()


def whole(dy, ids_t, hidden, gate_t, wq, we_t):
    tokens, width = dy.shape
    held, rows, _ = wq.shape
    routes, hid = hidden.shape
    groups = lax.axis_size("expert")
    slots = held * CAP
    full = rows * NX
    dma = pltpu.SemaphoreType.DMA
    vm = pltpu.VMEM
    return pl.pallas_call(
        whole_kernel,
        out_shape=(
            jax.ShapeDtypeStruct((routes, hid), BF),
            jax.ShapeDtypeStruct(gate_t.shape, F32),
            jax.ShapeDtypeStruct((held, rows // 2, width), F32),
        ),
        in_specs=[VMEM] * 6,
        out_specs=(VMEM,) * 3,
        scratch_shapes=[
            vm((groups * tokens, width), BF),
            vm((groups,) + ids_t.shape, jnp.int32),
            vm((groups, slots, hid), BF),
            vm((groups, slots, hid), BF),
            vm((held, full, width), BF),
            vm((held, groups * CAP, width), BF),
            vm((held, hid, groups * CAP), BF),
            vm((held, rows, width), F32),
            vm((NX - 1, held, rows, width), BF),
            vm((groups, slots, hid), BF),
            vm((2 * NZL, slots, hid), BF),
            vm((2 * NZL, slots, hid), BF),
            vm((held, rows // 2, width), BF),
            vm((held, rows // 2, width), BF),
            vm((held, rows // 2, width), BF),
            vm((held, groups, tokens), F32),
            vm((hid, 256), F32),
            dma((2, 15)), dma((2, 32)), dma((16,)), dma((32,)), dma((31,)), dma((32,)),
            dma((held, 32)), dma((held, 32)), dma((3,)), dma((4,)), dma((held, 32)), dma((held, 32)),
            dma((2, 2, 3)), dma((2, 2, 3)), dma((2, held)), dma((2, 2, 2)), dma((2, 2, 2)), dma((4,)),
        ],
        compiler_params=pltpu.CompilerParams(
            has_side_effects=True, vmem_limit_bytes=67043328, collective_id=0
        ),
        name="whole",
    )(dy, ids_t, hidden, gate_t, wq, we_t)


def body(
    out_grad, hidden_saved, gate_probs, expert_ids, weight_q, weight_exp, master, moment1, moment2
):
    tokens, top = expert_ids.shape
    hid = hidden_saved.shape[2]
    routes = tokens * top

    hidden_grad, gate_grad, gradient = whole(
        out_grad,
        expert_ids.T,
        hidden_saved.reshape(routes, hid),
        gate_probs.T,
        weight_q,
        weight_exp.transpose(0, 2, 1),
    )
    first = 0.9 * moment1.astype(F32) + 0.1 * gradient
    second = 0.95 * moment2.astype(F32) + 0.05 * gradient * gradient
    update = first / (1.0 - 0.9**20) / (jnp.sqrt(second / (1.0 - 0.95**20)) + 1e-08) + 0.1 * master
    return (
        hidden_grad.reshape(tokens, top, hid),
        gate_grad.T,
        master - 0.001 * update,
        first.astype(BF),
        second.astype(BF),
    )


def solution(mesh):
    tok = ("expert", "fsdp", "replica")
    in_specs = (
        P(tok, None),
        P(tok, None, None),
        P(tok, None),
        P(tok, None),
        P("expert", "fsdp", None),
        P("expert", "fsdp", None),
        P("expert", ("fsdp", "replica"), None),
        P("expert", ("fsdp", "replica"), None),
        P("expert", ("fsdp", "replica"), None),
    )
    out_specs = (
        P(tok, None, None),
        P(tok, None),
        P("expert", ("fsdp", "replica"), None),
        P("expert", ("fsdp", "replica"), None),
        P("expert", ("fsdp", "replica"), None),
    )
    return jax.shard_map(body, mesh=mesh, in_specs=in_specs, out_specs=out_specs, check_vma=False)
```

```python
import jax
import jax.numpy as jnp
from jax import lax
from jax.experimental import pallas as pl
from jax.experimental.pallas import tpu as pltpu
from jax.sharding import PartitionSpec as P

MESH = pl.DeviceIdType.MESH
NY, NZ, NZL, NX = 4, 8, 4, 4
CAP = 32
NP = 4
ORDER = (
    "V W0 g0", "g1 B0 O0", "r0 g2 r1", "g3 R0 P0", "W1 r2 g4", "R1 Z0 B1",
    "O1 r3 g5", "R2 Z1 r4", "g6 R3 Z2", "r5 g7 R4", "Z3 P1 r6", "R5 Z4 r7",
    "R6 Z5 R7", "Z6 Z7 D", "C04 F0 F1", "F2 F3 F4", "F5 F6 F7",
)
F32, BF = jnp.float32, jnp.bfloat16
ANY = pl.BlockSpec(memory_space=pl.ANY)
VMEM = pl.BlockSpec(memory_space=pltpu.VMEM)


class Place:
    def __init__(self):
        self.own = lax.axis_index("expert")
        self.core = lax.rem(self.own, 2)
        self.y = self.own // (2 * NZL)
        self.half = lax.axis_index("replica")
        self.z = self.half * NZL + lax.rem(self.own // 2, NZL)
        self.x = lax.axis_index("fsdp")
        self.s = 1 - 2 * self.core

    def slot(self, dy, dz, core):
        y = lax.rem(self.y + dy + NY, NY)
        zl = lax.rem(self.z + dz + NZ, NZL)
        return (y * NZL + zl) * 2 + core

    def dev(self, dy, dz, core):
        return {
            "expert": self.slot(dy, dz, core),
            "replica": lax.rem(self.z + dz + NZ, NZ) // NZL,
        }

    def dev_x(self, dx):
        return {"fsdp": lax.rem(self.x + dx + NX, NX)}

    def around(self, i):
        return self.s * ((1 - i % 2) * (i // 2) - (i % 2) * ((i + 1) // 2))


def remote(src, dst, ssem, rsem, dev):
    return pltpu.make_async_remote_copy(
        src_ref=src, dst_ref=dst, send_sem=ssem, recv_sem=rsem, device_id=dev, device_id_type=MESH
    )


def peers(p, far):
    out = []
    for dy in (1, -1, 0):
        for kind in (2, 1, 3, 0):
            for dc in (0, 1):
                core = p.core if dc == 0 else 1 - p.core
                if dc == 0 and dy == 0 and kind == 0:
                    continue
                dz = (0, 1, far(core), -1)[kind]
                out.append((p.dev(dy, dz, core), dy))
    return out


def far_row(p, dy, far):
    return [
        p.dev(dy, (0, 1, far(c), -1)[kind], c)
        for kind in range(NZL)
        for c in (p.core, 1 - p.core)
    ]


def spread(rows):
    k, t = rows.shape
    wide = jnp.broadcast_to(rows[None], (t, k, t)).reshape(t * k, t)
    at_t = lax.broadcasted_iota(jnp.int32, (t * k, t), 0) // k
    here = at_t == lax.broadcasted_iota(jnp.int32, (t * k, t), 1)
    return jnp.sum(jnp.where(here, wide, jnp.zeros_like(wide)), axis=1, keepdims=True)


def before(n):
    row = lax.broadcasted_iota(jnp.int32, (n, n), 0)
    return (row < lax.broadcasted_iota(jnp.int32, (n, n), 1)).astype(F32).astype(BF)


def whole_kernel(
    dy_ref, ids_t_ref, hid_ref, gate_ref, wq_ref, we_ref,
    hg_ref, gg_ref, gs_ref,
    rdy, rids, rw, ws, wf, xs, wt, own_g, rg, rback, b_via, d_via, ez_s, ez_t, ez_r, code, g_tile,
    dy_ss, dy_rs, sib_ss, sib_rs, id_ss, id_rs, b_ss, b_rs, w_ss, w_rs, d_ss, d_rs, e_ss, e_rs,
    v_rs, z_ss, z_rs, l_sem,
):
    p = Place()
    core, s = p.core, p.s
    tokens, width = dy_ref.shape
    held, rows, _ = wq_ref.shape
    routes, hid = hid_ref.shape
    groups = rids.shape[0]
    half = tokens // 2
    slots = held * CAP
    early, dys = [], []
    count = [0, 0, 0]

    def start(c, to):
        c.start()
        to.append(c)

    def part(slot, h):
        return rdy.at[pl.ds(pl.multiple_of(slot * tokens + h * half, half), half)]

    def block(slot):
        return rdy.at[pl.ds(pl.multiple_of(slot * tokens, tokens), tokens)]

    def at(h, a, b):
        return (a, b) if h == 0 else (b, a)

    def send_dy(src, slot, h, dev):
        k = count[h]
        count[h] += 1
        start(remote(src, part(slot, h), dy_ss.at[h, k], dy_rs.at[h, slot], dev), dys)

    def wait_dy(slot, h):
        blk = part(slot, h)
        remote(blk, blk, dy_ss.at[h, 0], dy_rs.at[h, slot], p.dev(1, 0, core)).wait_recv()

    def send_sib(src, slot):
        k = count[2]
        count[2] += 1
        start(remote(src, block(slot), sib_ss.at[k], sib_rs.at[slot], p.dev(0, 0, 1 - core)), dys)

    def wait_sib(slot):
        blk = block(slot)
        remote(blk, blk, sib_ss.at[0], sib_rs.at[slot], p.dev(0, 0, 1 - core)).wait_recv()

    gate = pltpu.get_barrier_semaphore()
    near = [dev for dev, _ in peers(p, lambda c: 2 * s)] + far_row(p, 2, lambda c: 2 * s)
    near += [p.dev(dy, -2 * s, core) for dy in range(NY)]
    near += [p.dev_x(d) for d in (1, 2, 3)] + [{"replica": 1 - p.half}]
    for dev in near:
        pl.semaphore_signal(gate, inc=1, device_id=dev, device_id_type=MESH)
    pl.semaphore_wait(gate, len(near))

    def mine(h):
        return dy_ref.at[pl.ds(h * half, half)]

    for h in (0, 1):
        for d in (1, -1):
            send_dy(mine(h), p.own, h, p.dev(*at(h, d, 0), core))
    for h in (0, 1):
        for d in (1, -1):
            send_dy(mine(h), p.own, h, p.dev(*at(h, 0, d), core))
    send_sib(dy_ref, p.own)
    there = peers(p, lambda c: 2 * s)
    for k, dev in enumerate([dev for dev, _ in there] + far_row(p, 2, lambda c: 2 * s)):
        start(remote(ids_t_ref, rids.at[p.own], id_ss.at[k], id_rs.at[p.own], dev), early)
    local = [
        pltpu.make_async_copy(dy_ref, block(p.own), l_sem.at[0]),
        pltpu.make_async_copy(ids_t_ref, rids.at[p.own], l_sem.at[1]),
    ]
    for c in local:
        c.start()

    def shard(x):
        return wf.at[:, pl.ds(pl.multiple_of(x * rows, rows), rows)]

    mine_w = pl.ds(pl.multiple_of(p.x * rows, rows), rows)
    qb = width // we_ref.shape[1]
    for e in range(held):
        blocks = we_ref.shape[1]
        same = lax.broadcasted_iota(jnp.int32, (blocks, blocks), 0) == lax.broadcasted_iota(
            jnp.int32, (blocks, blocks), 1
        )
        power = lax.dot_general(
            we_ref[e].astype(F32).astype(BF), same.astype(F32).astype(BF),
            (((0,), (0,)), ((), ())), preferred_element_type=F32,
        )
        scale = jnp.exp2(power)
        for j in range(blocks):
            cols = pl.ds(j * qb, qb)
            wf[e, mine_w, cols] = (wq_ref[e, :, cols].astype(F32) * scale[:, j : j + 1]).astype(BF)

    experts = groups * held
    ids_t = ids_t_ref[...]
    top = ids_t.shape[0]
    expert = lax.broadcasted_iota(jnp.int32, (experts, tokens), 0)
    named = jnp.zeros((experts, tokens), F32)
    for k in range(top):
        named += (ids_t[k : k + 1] == expert).astype(F32)
    rank = jnp.dot(named.astype(BF), before(tokens), preferred_element_type=F32)
    rank_t = jnp.concatenate(
        [
            jnp.sum(jnp.where(ids_t[k : k + 1] == expert, rank, 0.0), axis=0, keepdims=True)
            for k in range(top)
        ],
        axis=0,
    )
    slot_t = ids_t * CAP + rank_t.astype(jnp.int32)
    both = jnp.concatenate([ids_t.astype(F32), rank_t], axis=0).astype(BF)
    lane_t = lax.broadcasted_iota(jnp.int32, (tokens, routes), 1) // top
    over = (lane_t == lax.broadcasted_iota(jnp.int32, (tokens, routes), 0)).astype(F32)
    both = jnp.dot(both, over.astype(BF), preferred_element_type=F32)
    mine_k = lax.rem(
        lax.broadcasted_iota(jnp.int32, (top, routes), 1), top
    ) == lax.broadcasted_iota(jnp.int32, (top, routes), 0)
    slot_row = jnp.sum(
        jnp.where(mine_k, both[:top] * CAP + both[top:], 0.0), axis=0, keepdims=True
    ).astype(jnp.int32)
    hg_ref[...] = (spread(gate_ref[...]) * hid_ref[...].astype(F32)).astype(BF)

    for i, dx in enumerate((1, -1)):
        start(remote(shard(p.x), shard(p.x), w_ss.at[i], w_rs.at[p.x], p.dev_x(dx)), early)

    step = 256
    per = step // slots

    def fill(i, _):
        lo = i * step
        pick = (slot_row == lax.broadcasted_iota(jnp.int32, (step, routes), 0) + lo).astype(F32)
        got = jnp.dot(pick.astype(BF), hg_ref[...], preferred_element_type=F32).astype(BF)
        ws[pl.ds(i * per, per)] = got.reshape(per, slots, hid)
        return 0

    lax.fori_loop(0, groups // per, fill, 0)

    for h in (0, 1):
        b = p.slot(*at(h, -s, 0), core)
        wait_dy(b, h)
        send_dy(part(b, h), b, h, p.dev(*at(h, s, 0), core))
        for d in (1, -1):
            send_dy(part(b, h), b, h, p.dev(*at(h, 0, d), core))

    def of_expert(ref, j, e):
        return ref.at[j, pl.ds(e * CAP, CAP)]

    row_sends = [[] for _ in range(held)]

    def far_rows(ref, e, y):
        y = lax.rem(y + 2 * NY, NY)
        return ref.at[pl.ds(y * 2 * NZL, 2 * NZL), pl.ds(e * CAP, CAP)]

    def send_rows(e):
        far = far_rows(ws, e, p.y + 2)
        via = b_via.at[:, pl.ds(e * CAP, CAP)]
        start(remote(far, via, b_ss.at[e, 31], v_rs.at[0, e], p.dev(s, 0, core)), row_sends[e])
        for k in range(23):
            dev = there[k][0]
            src, dst = of_expert(ws, dev["expert"], e), of_expert(rw, p.own, e)
            start(remote(src, dst, b_ss.at[e, k], b_rs.at[e, p.own], dev), row_sends[e])

    def pass_rows(via, dst, e, k, ss, rs, far, to):
        blk = via.at[:, pl.ds(e * CAP, CAP)]
        remote(blk, blk, ss.at[e, 31], v_rs.at[k, e], p.dev(s, 0, core)).wait_recv()
        origin = p.slot(-s, 0, core)
        for i, dev in enumerate(far_row(p, s, far)):
            src = of_expert(via, lax.rem(dev["expert"], 2 * NZL), e)
            start(
                remote(src, of_expert(dst, origin, e), ss.at[e, 23 + i], rs.at[e, origin], dev), to
            )

    own_rows = pltpu.make_async_copy(ws.at[p.own], rw.at[p.own], l_sem.at[2])
    own_rows.start()
    send_rows(0)
    for a in (s, -2 * s):
        for h in (0, 1):
            b = p.slot(*at(h, a, 0), core)
            wait_dy(b, h)
            for d in (1, -1):
                send_dy(part(b, h), b, h, p.dev(*at(h, 0, d), core))
    pass_rows(b_via, rw, 0, 0, b_ss, b_rs, lambda c: 2 * s, row_sends[0])
    for a in (0, -s, s, -2 * s):
        for h in (0, 1):
            b = p.slot(*at(h, a, -s), core)
            wait_dy(b, h)
            send_dy(part(b, h), b, h, p.dev(*at(h, 0, s), core))
    send_rows(1)

    back_x = lax.rem(p.x - s + NX, NX)
    remote(shard(back_x), shard(back_x), w_ss.at[2], w_rs.at[back_x], p.dev_x(s)).wait_recv()
    start(remote(shard(back_x), shard(back_x), w_ss.at[2], w_rs.at[back_x], p.dev_x(s)), early)

    local[1].wait()
    for dc in (0, 1):
        c2 = core if dc == 0 else 1 - core
        for dy in range(NY):
            for dz in range(NZL):
                if dc == 0 and dy == 0 and dz == 0:
                    continue
                j = p.slot(dy, dz, c2)
                remote(
                    rids.at[j], rids.at[j], id_ss.at[0], id_rs.at[j], p.dev(1, 0, core)
                ).wait_recv()
    tri = before(tokens)
    for e in range(held):
        hit = jnp.sum((rids[...] == p.own * held + e).astype(F32), axis=1)
        code[e] = jnp.where(
            hit > 0, jnp.dot(hit.astype(BF), tri, preferred_element_type=F32), -1.0
        )

    def pick_rows(j):
        lane = lax.broadcasted_iota(jnp.int32, (CAP, tokens), 0).astype(F32)
        pick = jnp.concatenate(
            [(code[e, pl.ds(j, 1), :] == lane).astype(F32) for e in range(held)], axis=0
        ).astype(BF)
        got = jnp.dot(pick, block(j)[...], preferred_element_type=F32).astype(BF)
        for e in range(held):
            xs[e, pl.ds(pl.multiple_of(j * CAP, CAP), CAP)] = got[e * CAP : (e + 1) * CAP]

    def pair(g, k):
        t = g // (k + 1)
        return (1 - t) * g + t * k, (1 - t) * k + t * (g - k - 1)

    def own_stage(k):
        offs = (0, -s, s, -2 * s)
        pairs = [(i, k) for i in range(k)] + [(k, j) for j in range(k)] + [(k, k)]
        for i, j in pairs:
            b = p.slot(offs[i], offs[j], core)
            if j > 1:
                wait_dy(b, 0)
            if i > 1:
                wait_dy(b, 1)
            send_sib(block(b), b)

        def one(g, _):
            i, j = pair(g, k)
            pick_rows(p.slot(p.around(i), p.around(j), core))
            return 0

        lax.fori_loop(0, 2 * k + 1, one, 0)

    def sib_stage(k):
        def one(g, _):
            i, j = pair(g, k)
            b = p.slot(-p.around(i), -p.around(j), 1 - core)
            wait_sib(b)
            pick_rows(b)
            return 0

        lax.fori_loop(0, 2 * k + 1, one, 0)

    local[0].wait()
    pick_rows(p.own)
    own_stage(1)
    sib_stage(0)
    own_stage(2)
    pass_rows(b_via, rw, 1, 0, b_ss, b_rs, lambda c: 2 * s, row_sends[1])
    sib_stage(1)
    own_stage(3)
    sib_stage(2)
    sib_stage(3)

    for c in dys:
        c.wait_send()
    own_rows.wait()

    def others():
        for dc in (0, 1):
            c2 = core if dc == 0 else 1 - core
            for dy in range(NY):
                for dz in range(NZL):
                    if dc or dy or dz:
                        yield p.slot(dy, dz, c2)

    chunk = groups * CAP // 4
    piece = width // NP
    nt = 256
    late = []

    def rows_of(e, x):
        x = lax.rem(x + 2 * NX, NX)
        return pl.ds(pl.multiple_of(e * hid + x * rows, rows), rows)

    def weighted_here(e):
        for j in others():
            a = of_expert(rw, j, e)
            remote(a, a, b_ss.at[e, 0], b_rs.at[e, j], p.dev(1, 0, core)).wait_recv()
        for c in row_sends[e]:
            c.wait_send()
        for i in range(4):
            got = rw[i * 8 : (i + 1) * 8, e * CAP : (e + 1) * CAP].reshape(chunk, hid)
            wt[e, :, i * chunk : (i + 1) * chunk] = got.T

    def to_x(e, h, k, x, dx):
        cols = pl.ds(h * piece, piece)
        src = rdy.at[rows_of(e, x), cols]
        dst = rg.at[k, e, :, cols]
        start(remote(src, dst, e_ss.at[e, h, k], e_rs.at[e, h, k], p.dev_x(dx)), late)

    def from_x(e, h, k):
        a = rg.at[k, e, :, pl.ds(h * piece, piece)]
        remote(a, a, e_ss.at[e, h, k], e_rs.at[e, h, k], p.dev_x(1)).wait_recv()

    def grad_piece(e, h):
        def tile(n, _):
            cols = pl.ds(pl.multiple_of(h * piece + n * nt, nt), nt)
            g = jnp.dot(wt[e], xs[e, :, cols], preferred_element_type=F32)
            rdy[e * hid : (e + 1) * hid, cols] = g.astype(BF)
            g_tile[...] = g
            own_g[e, :, cols] = g_tile[mine_w]
            return 0

        lax.fori_loop(0, piece // nt, tile, 0)
        to_x(e, h, 0, p.x + 2 * s, s)
        to_x(e, h, 1, p.x - s, -s)

    def relay_piece(e, h):
        cols = pl.ds(h * piece, piece)
        from_x(e, h, 0)
        r = rows_of(e, p.x + s)
        rdy[r, cols] = (rdy[r, cols].astype(F32) + rg[0, e, :, cols].astype(F32)).astype(BF)
        to_x(e, h, 2, p.x + s, s)

    back_at = held * hid

    def back_of(e, j, n):
        at_j = pl.multiple_of(back_at + e * groups * CAP + j * CAP, CAP)
        return rdy.at[pl.ds(at_j, n * CAP), pl.ds(0, hid)]

    def back_tile(e, dy):
        yy = lax.rem(p.y + dy + NY, NY)
        x_rows = xs[e, pl.ds(pl.multiple_of(yy * 256, 256), 256)]
        got = lax.dot_general(x_rows, wf[e], (((1,), (1,)), ((), ())), preferred_element_type=F32)
        to = pl.multiple_of(back_at + e * groups * CAP + yy * 256, 256)
        rdy[pl.ds(to, 256), :hid] = got.astype(BF)

    home = peers(p, lambda c: 4 * c - 2)

    def back_rows(e):
        for dy in (2, 1, -1, 0):
            back_tile(e, dy)
            if dy == 2:
                far = back_of(e, lax.rem(p.y + 2, NY) * 2 * NZL, 2 * NZL)
                c = remote(far, d_via.at[e], d_ss.at[e, 31], v_rs.at[1, e], p.dev(s, 0, core))
                start(c, late)
            for k, (dev, dy2) in enumerate(home):
                if dy2 == dy:
                    src, dst = back_of(e, dev["expert"], 1), of_expert(rback, p.own, e)
                    start(remote(src, dst, d_ss.at[e, k], d_rs.at[e, p.own], dev), late)

    def pass_back(e):
        blk = d_via.at[e]
        remote(blk, blk, d_ss.at[e, 31], v_rs.at[1, e], p.dev(s, 0, core)).wait_recv()
        origin = p.slot(-s, 0, core)
        for i, dev in enumerate(far_row(p, s, lambda c: 4 * c - 2)):
            j = lax.rem(dev["expert"], 2 * NZL)
            src = d_via.at[e, pl.ds(pl.multiple_of(j * CAP, CAP), CAP)]
            dst = of_expert(rback, origin, e)
            start(remote(src, dst, d_ss.at[e, 23 + i], d_rs.at[e, origin], dev), late)

    keep = rows // 2

    def to_z(src, dst, k, e, h):
        cols = pl.ds(h * piece, piece)
        c = remote(
            src.at[e, :, cols], dst.at[e, :, cols], z_ss.at[k, e, h], z_rs.at[k, e, h],
            p.dev(0, 2 * s, core),
        )
        start(c, late)

    def from_z(dst, k, e, h):
        a = dst.at[e, :, pl.ds(h * piece, piece)]
        remote(a, a, z_ss.at[k, e, h], z_rs.at[k, e, h], p.dev(0, 2 * s, core)).wait_recv()

    def pass_z(e, h):
        from_z(ez_t, 0, e, h)
        to_z(ez_t, ez_r, 1, e, h)

    def reduce_piece(e, h):
        cols = pl.ds(h * piece, piece)
        from_x(e, h, 1)
        from_x(e, h, 2)

        def total(r):
            at_r = pl.ds(pl.multiple_of(r * keep, keep), keep)
            t = own_g[e, at_r, cols]
            for k in (1, 2):
                t += rg[k, e, at_r, cols].astype(F32)
            return t

        ez_s[e, :, cols] = total(1 - p.half).astype(BF)
        gs_ref[e, :, cols] = total(p.half)
        to_z(ez_s, ez_t, 0, e, h)

    tk = step // top
    sub = lax.broadcasted_iota(jnp.int32, (step, tokens), 0) // top
    lane = lax.broadcasted_iota(jnp.int32, (step, tokens), 1)

    def join(i, _):
        r = pl.ds(pl.multiple_of(i * step, step), step)
        here = sub + i * tk == lane

        def column(rows):
            wide = jnp.broadcast_to(rows[None], (tk, top, tokens)).reshape(step, tokens)
            return jnp.sum(jnp.where(here, wide, jnp.zeros_like(wide)), axis=1, keepdims=True)

        pick = column(slot_t) == lax.broadcasted_iota(jnp.int32, (step, groups * slots), 1)
        got = jnp.dot(
            pick.astype(F32).astype(BF),
            rback[...].reshape(groups * slots, hid),
            preferred_element_type=F32,
        )
        hg_ref[r] = (column(gate_ref[...]) * got).astype(BF)
        dots = jnp.sum(hid_ref[r].astype(F32) * got, axis=1, keepdims=True)
        gg_ref[...] += jnp.sum(
            jnp.where(here, dots, 0.0).reshape(tk, top, tokens), axis=0
        )
        return 0

    def joins(lo, hi):
        lax.fori_loop(lo, hi, join, 0)

    def whole_weights():
        for dx in (1, 2):
            j = lax.rem(p.x + dx * s + 2 * NX, NX)
            remote(shard(j), shard(j), w_ss.at[0], w_rs.at[j], p.dev_x(1)).wait_recv()

    def returned():
        for c in own_back:
            c.wait()
        for j in others():
            for e in range(held):
                a = of_expert(rback, j, e)
                remote(a, a, d_ss.at[e, 0], d_rs.at[e, j], p.dev(1, 0, core)).wait_recv()

    def finish(e, h):
        cols = pl.ds(h * piece, piece)
        from_z(ez_r, 1, e, h)
        gs_ref[e, :, cols] += ez_r[e, :, cols].astype(F32)

    gg_ref[...] = jnp.zeros_like(gg_ref)
    own_back = [
        pltpu.make_async_copy(back_of(e, p.own, 1), of_expert(rback, p.own, e), l_sem.at[2 + e])
        for e in range(held)
    ]
    steps = {
        "g": grad_piece, "r": relay_piece, "R": reduce_piece, "Z": pass_z, "F": finish,
    }
    for word in " ".join(ORDER).split():
        if word[0] in steps:
            steps[word[0]](int(word[1:]) // NP, int(word[1:]) % NP)
        elif word[0] == "W":
            weighted_here(int(word[1]))
        elif word == "V":
            whole_weights()
        elif word[0] == "B":
            back_rows(int(word[1]))
        elif word[0] == "P":
            pass_back(int(word[1]))
        elif word[0] == "O":
            own_back[int(word[1])].start()
        elif word == "D":
            returned()
        elif word[0] == "C":
            joins(int(word[1]), int(word[2]))
    for c in early + late:
        c.wait_send()


def whole(dy, ids_t, hidden, gate_t, wq, we_t):
    tokens, width = dy.shape
    held, rows, _ = wq.shape
    routes, hid = hidden.shape
    groups = lax.axis_size("expert")
    slots = held * CAP
    full = rows * NX
    dma = pltpu.SemaphoreType.DMA
    vm = pltpu.VMEM
    return pl.pallas_call(
        whole_kernel,
        out_shape=(
            jax.ShapeDtypeStruct((routes, hid), BF),
            jax.ShapeDtypeStruct(gate_t.shape, F32),
            jax.ShapeDtypeStruct((held, rows // 2, width), F32),
        ),
        in_specs=[VMEM] * 6,
        out_specs=(VMEM,) * 3,
        scratch_shapes=[
            vm((groups * tokens, width), BF),
            vm((groups,) + ids_t.shape, jnp.int32),
            vm((groups, slots, hid), BF),
            vm((groups, slots, hid), BF),
            vm((held, full, width), BF),
            vm((held, groups * CAP, width), BF),
            vm((held, hid, groups * CAP), BF),
            vm((held, rows, width), F32),
            vm((NX - 1, held, rows, width), BF),
            vm((groups, slots, hid), BF),
            vm((2 * NZL, slots, hid), BF),
            vm((held, 2 * NZL * CAP, hid), BF),
            vm((held, rows // 2, width), BF),
            vm((held, rows // 2, width), BF),
            vm((held, rows // 2, width), BF),
            vm((held, groups, tokens), F32),
            vm((hid, 256), F32),
            dma((2, 15)), dma((2, 32)), dma((16,)), dma((32,)), dma((31,)), dma((32,)),
            dma((held, 32)), dma((held, 32)), dma((3,)), dma((4,)), dma((held, 32)), dma((held, 32)),
            dma((held, NP, 3)), dma((held, NP, 3)), dma((2, held)), dma((2, held, NP)), dma((2, held, NP)), dma((4,)),
        ],
        compiler_params=pltpu.CompilerParams(
            has_side_effects=True, vmem_limit_bytes=67043328, collective_id=0
        ),
        name="whole",
    )(dy, ids_t, hidden, gate_t, wq, we_t)


def body(
    out_grad, hidden_saved, gate_probs, expert_ids, weight_q, weight_exp, master, moment1, moment2
):
    tokens, top = expert_ids.shape
    hid = hidden_saved.shape[2]
    routes = tokens * top

    hidden_grad, gate_grad, gradient = whole(
        out_grad,
        expert_ids.T,
        hidden_saved.reshape(routes, hid),
        gate_probs.T,
        weight_q,
        weight_exp.transpose(0, 2, 1),
    )
    first = 0.9 * moment1.astype(F32) + 0.1 * gradient
    second = 0.95 * moment2.astype(F32) + 0.05 * gradient * gradient
    update = first / (1.0 - 0.9**20) / (jnp.sqrt(second / (1.0 - 0.95**20)) + 1e-08) + 0.1 * master
    return (
        hidden_grad.reshape(tokens, top, hid),
        gate_grad.T,
        master - 0.001 * update,
        first.astype(BF),
        second.astype(BF),
    )


def solution(mesh):
    tok = ("expert", "fsdp", "replica")
    in_specs = (
        P(tok, None),
        P(tok, None, None),
        P(tok, None),
        P(tok, None),
        P("expert", "fsdp", None),
        P("expert", "fsdp", None),
        P("expert", ("fsdp", "replica"), None),
        P("expert", ("fsdp", "replica"), None),
        P("expert", ("fsdp", "replica"), None),
    )
    out_specs = (
        P(tok, None, None),
        P(tok, None),
        P("expert", ("fsdp", "replica"), None),
        P("expert", ("fsdp", "replica"), None),
        P("expert", ("fsdp", "replica"), None),
    )
    return jax.shard_map(body, mesh=mesh, in_specs=in_specs, out_specs=out_specs, check_vma=False)
```

```python
import jax
import jax.numpy as jnp
from jax import lax
from jax.experimental import pallas as pl
from jax.experimental.pallas import tpu as pltpu
from jax.sharding import PartitionSpec as P

MESH = pl.DeviceIdType.MESH
NY, NZ, NZL, NX = 4, 8, 4, 4
CAP = 32
NP = 4
ORDER = (
    "V W0 g0", "g1 B0 O0", "r0 g2 r1", "g3 R0 P0", "W1 r2 g4", "R1 B1 O1",
    "r3 g5 R2", "Z0 r4 g6", "R3 Z1 r5", "g7 R4 Z2", "P1 r6 R5", "Z3 r7 R6",
    "Z4 R7 Z5", "Z6 D C02", "Z7 C24 F0", "F1 F2 F3", "F4 F5 F6", "F7",
)
F32, BF = jnp.float32, jnp.bfloat16
ANY = pl.BlockSpec(memory_space=pl.ANY)
VMEM = pl.BlockSpec(memory_space=pltpu.VMEM)


class Place:
    def __init__(self):
        self.own = lax.axis_index("expert")
        self.core = lax.rem(self.own, 2)
        self.y = self.own // (2 * NZL)
        self.half = lax.axis_index("replica")
        self.z = self.half * NZL + lax.rem(self.own // 2, NZL)
        self.x = lax.axis_index("fsdp")
        self.s = 1 - 2 * self.core

    def slot(self, dy, dz, core):
        y = lax.rem(self.y + dy + NY, NY)
        zl = lax.rem(self.z + dz + NZ, NZL)
        return (y * NZL + zl) * 2 + core

    def dev(self, dy, dz, core):
        return {
            "expert": self.slot(dy, dz, core),
            "replica": lax.rem(self.z + dz + NZ, NZ) // NZL,
        }

    def dev_x(self, dx):
        return {"fsdp": lax.rem(self.x + dx + NX, NX)}

    def around(self, i):
        return self.s * ((1 - i % 2) * (i // 2) - (i % 2) * ((i + 1) // 2))


def remote(src, dst, ssem, rsem, dev):
    return pltpu.make_async_remote_copy(
        src_ref=src, dst_ref=dst, send_sem=ssem, recv_sem=rsem, device_id=dev, device_id_type=MESH
    )


def peers(p, far):
    out = []
    for dy in (1, -1, 0):
        for kind in (2, 1, 3, 0):
            for dc in (0, 1):
                core = p.core if dc == 0 else 1 - p.core
                if dc == 0 and dy == 0 and kind == 0:
                    continue
                dz = (0, 1, far(core), -1)[kind]
                out.append((p.dev(dy, dz, core), dy))
    return out


def far_row(p, dy, far):
    return [
        p.dev(dy, (0, 1, far(c), -1)[kind], c)
        for kind in range(NZL)
        for c in (p.core, 1 - p.core)
    ]


def spread(rows):
    k, t = rows.shape
    wide = jnp.broadcast_to(rows[None], (t, k, t)).reshape(t * k, t)
    at_t = lax.broadcasted_iota(jnp.int32, (t * k, t), 0) // k
    here = at_t == lax.broadcasted_iota(jnp.int32, (t * k, t), 1)
    return jnp.sum(jnp.where(here, wide, jnp.zeros_like(wide)), axis=1, keepdims=True)


def before(n):
    row = lax.broadcasted_iota(jnp.int32, (n, n), 0)
    return (row < lax.broadcasted_iota(jnp.int32, (n, n), 1)).astype(F32).astype(BF)


def whole_kernel(
    dy_ref, ids_t_ref, hid_in, gate_ref, wq_in, we_ref,
    hg_ref, gg_ref, gs_ref,
    rdy, rids, rw, ws, wf, xs, wt, own_g, rg, rback, b_via, d_via, ez_s, ez_t, ez_r, code, g_tile, hid_ref, wq_ref,
    dy_ss, dy_rs, sib_ss, sib_rs, id_ss, id_rs, b_ss, b_rs, w_ss, w_rs, d_ss, d_rs, e_ss, e_rs,
    v_rs, z_ss, z_rs, l_sem,
):
    p = Place()
    core, s = p.core, p.s
    tokens, width = dy_ref.shape
    held, rows, _ = wq_ref.shape
    routes, hid = hid_ref.shape
    groups = rids.shape[0]
    half = tokens // 2
    slots = held * CAP
    early, dys = [], []
    count = [0, 0, 0]

    def start(c, to):
        c.start()
        to.append(c)

    def part(slot, h):
        return rdy.at[pl.ds(pl.multiple_of(slot * tokens + h * half, half), half)]

    def block(slot):
        return rdy.at[pl.ds(pl.multiple_of(slot * tokens, tokens), tokens)]

    def at(h, a, b):
        return (a, b) if h == 0 else (b, a)

    def send_dy(src, slot, h, dev):
        k = count[h]
        count[h] += 1
        start(remote(src, part(slot, h), dy_ss.at[h, k], dy_rs.at[h, slot], dev), dys)

    def wait_dy(slot, h):
        blk = part(slot, h)
        remote(blk, blk, dy_ss.at[h, 0], dy_rs.at[h, slot], p.dev(1, 0, core)).wait_recv()

    def send_sib(src, slot):
        k = count[2]
        count[2] += 1
        start(remote(src, block(slot), sib_ss.at[k], sib_rs.at[slot], p.dev(0, 0, 1 - core)), dys)

    def wait_sib(slot):
        blk = block(slot)
        remote(blk, blk, sib_ss.at[0], sib_rs.at[slot], p.dev(0, 0, 1 - core)).wait_recv()

    loads = [
        pltpu.make_async_copy(wq_in, wq_ref, l_sem.at[4]),
        pltpu.make_async_copy(hid_in, hid_ref, l_sem.at[5]),
    ]
    for c in loads:
        c.start()

    gate = pltpu.get_barrier_semaphore()
    near = [dev for dev, _ in peers(p, lambda c: 2 * s)] + far_row(p, 2, lambda c: 2 * s)
    near += [p.dev(dy, -2 * s, core) for dy in range(NY)]
    near += [p.dev_x(d) for d in (1, 2, 3)] + [{"replica": 1 - p.half}]
    for dev in near:
        pl.semaphore_signal(gate, inc=1, device_id=dev, device_id_type=MESH)
    pl.semaphore_wait(gate, len(near))

    def mine(h):
        return dy_ref.at[pl.ds(h * half, half)]

    for h in (0, 1):
        for d in (1, -1):
            send_dy(mine(h), p.own, h, p.dev(*at(h, d, 0), core))
    for h in (0, 1):
        for d in (1, -1):
            send_dy(mine(h), p.own, h, p.dev(*at(h, 0, d), core))
    send_sib(dy_ref, p.own)
    there = peers(p, lambda c: 2 * s)
    for k, dev in enumerate([dev for dev, _ in there] + far_row(p, 2, lambda c: 2 * s)):
        start(remote(ids_t_ref, rids.at[p.own], id_ss.at[k], id_rs.at[p.own], dev), early)
    local = [
        pltpu.make_async_copy(dy_ref, block(p.own), l_sem.at[0]),
        pltpu.make_async_copy(ids_t_ref, rids.at[p.own], l_sem.at[1]),
    ]
    for c in local:
        c.start()

    def shard(x):
        return wf.at[:, pl.ds(pl.multiple_of(x * rows, rows), rows)]

    mine_w = pl.ds(pl.multiple_of(p.x * rows, rows), rows)
    qb = width // we_ref.shape[1]
    loads[0].wait()
    for e in range(held):
        blocks = we_ref.shape[1]
        same = lax.broadcasted_iota(jnp.int32, (blocks, blocks), 0) == lax.broadcasted_iota(
            jnp.int32, (blocks, blocks), 1
        )
        power = lax.dot_general(
            we_ref[e].astype(F32).astype(BF), same.astype(F32).astype(BF),
            (((0,), (0,)), ((), ())), preferred_element_type=F32,
        )
        scale = jnp.exp2(power)
        for j in range(blocks):
            cols = pl.ds(j * qb, qb)
            wf[e, mine_w, cols] = (wq_ref[e, :, cols].astype(F32) * scale[:, j : j + 1]).astype(BF)

    experts = groups * held
    ids_t = ids_t_ref[...]
    top = ids_t.shape[0]
    expert = lax.broadcasted_iota(jnp.int32, (experts, tokens), 0)
    named = jnp.zeros((experts, tokens), F32)
    for k in range(top):
        named += (ids_t[k : k + 1] == expert).astype(F32)
    rank = jnp.dot(named.astype(BF), before(tokens), preferred_element_type=F32)
    rank_t = jnp.concatenate(
        [
            jnp.sum(jnp.where(ids_t[k : k + 1] == expert, rank, 0.0), axis=0, keepdims=True)
            for k in range(top)
        ],
        axis=0,
    )
    slot_t = ids_t * CAP + rank_t.astype(jnp.int32)
    both = jnp.concatenate([ids_t.astype(F32), rank_t], axis=0).astype(BF)
    lane_t = lax.broadcasted_iota(jnp.int32, (tokens, routes), 1) // top
    over = (lane_t == lax.broadcasted_iota(jnp.int32, (tokens, routes), 0)).astype(F32)
    both = jnp.dot(both, over.astype(BF), preferred_element_type=F32)
    mine_k = lax.rem(
        lax.broadcasted_iota(jnp.int32, (top, routes), 1), top
    ) == lax.broadcasted_iota(jnp.int32, (top, routes), 0)
    slot_row = jnp.sum(
        jnp.where(mine_k, both[:top] * CAP + both[top:], 0.0), axis=0, keepdims=True
    ).astype(jnp.int32)
    loads[1].wait()
    hg_ref[...] = (spread(gate_ref[...]) * hid_ref[...].astype(F32)).astype(BF)

    for i, dx in enumerate((1, -1)):
        start(remote(shard(p.x), shard(p.x), w_ss.at[i], w_rs.at[p.x], p.dev_x(dx)), early)

    step = 256
    per = step // slots

    def fill(i, _):
        lo = i * step
        pick = (slot_row == lax.broadcasted_iota(jnp.int32, (step, routes), 0) + lo).astype(F32)
        got = jnp.dot(pick.astype(BF), hg_ref[...], preferred_element_type=F32).astype(BF)
        ws[pl.ds(i * per, per)] = got.reshape(per, slots, hid)
        return 0

    lax.fori_loop(0, groups // per, fill, 0)

    for h in (0, 1):
        b = p.slot(*at(h, -s, 0), core)
        wait_dy(b, h)
        send_dy(part(b, h), b, h, p.dev(*at(h, s, 0), core))
        for d in (1, -1):
            send_dy(part(b, h), b, h, p.dev(*at(h, 0, d), core))

    def of_expert(ref, j, e):
        return ref.at[j, pl.ds(e * CAP, CAP)]

    row_sends = [[] for _ in range(held)]

    def far_rows(ref, e, y):
        y = lax.rem(y + 2 * NY, NY)
        return ref.at[pl.ds(y * 2 * NZL, 2 * NZL), pl.ds(e * CAP, CAP)]

    def send_rows(e):
        far = far_rows(ws, e, p.y + 2)
        via = b_via.at[:, pl.ds(e * CAP, CAP)]
        start(remote(far, via, b_ss.at[e, 31], v_rs.at[0, e], p.dev(s, 0, core)), row_sends[e])
        for k in range(23):
            dev = there[k][0]
            src, dst = of_expert(ws, dev["expert"], e), of_expert(rw, p.own, e)
            start(remote(src, dst, b_ss.at[e, k], b_rs.at[e, p.own], dev), row_sends[e])

    def pass_rows(via, dst, e, k, ss, rs, far, to):
        blk = via.at[:, pl.ds(e * CAP, CAP)]
        remote(blk, blk, ss.at[e, 31], v_rs.at[k, e], p.dev(s, 0, core)).wait_recv()
        origin = p.slot(-s, 0, core)
        for i, dev in enumerate(far_row(p, s, far)):
            src = of_expert(via, lax.rem(dev["expert"], 2 * NZL), e)
            start(
                remote(src, of_expert(dst, origin, e), ss.at[e, 23 + i], rs.at[e, origin], dev), to
            )

    own_rows = pltpu.make_async_copy(ws.at[p.own], rw.at[p.own], l_sem.at[2])
    own_rows.start()
    send_rows(0)
    for a in (s, -2 * s):
        for h in (0, 1):
            b = p.slot(*at(h, a, 0), core)
            wait_dy(b, h)
            for d in (1, -1):
                send_dy(part(b, h), b, h, p.dev(*at(h, 0, d), core))
    pass_rows(b_via, rw, 0, 0, b_ss, b_rs, lambda c: 2 * s, row_sends[0])
    for a in (0, -s, s, -2 * s):
        for h in (0, 1):
            b = p.slot(*at(h, a, -s), core)
            wait_dy(b, h)
            send_dy(part(b, h), b, h, p.dev(*at(h, 0, s), core))
    send_rows(1)

    back_x = lax.rem(p.x - s + NX, NX)
    remote(shard(back_x), shard(back_x), w_ss.at[2], w_rs.at[back_x], p.dev_x(s)).wait_recv()
    start(remote(shard(back_x), shard(back_x), w_ss.at[2], w_rs.at[back_x], p.dev_x(s)), early)

    local[1].wait()
    for dc in (0, 1):
        c2 = core if dc == 0 else 1 - core
        for dy in range(NY):
            for dz in range(NZL):
                if dc == 0 and dy == 0 and dz == 0:
                    continue
                j = p.slot(dy, dz, c2)
                remote(
                    rids.at[j], rids.at[j], id_ss.at[0], id_rs.at[j], p.dev(1, 0, core)
                ).wait_recv()
    tri = before(tokens)
    for e in range(held):
        hit = jnp.sum((rids[...] == p.own * held + e).astype(F32), axis=1)
        code[e] = jnp.where(
            hit > 0, jnp.dot(hit.astype(BF), tri, preferred_element_type=F32), -1.0
        )

    def pick_rows(j):
        lane = lax.broadcasted_iota(jnp.int32, (CAP, tokens), 0).astype(F32)
        pick = jnp.concatenate(
            [(code[e, pl.ds(j, 1), :] == lane).astype(F32) for e in range(held)], axis=0
        ).astype(BF)
        got = jnp.dot(pick, block(j)[...], preferred_element_type=F32).astype(BF)
        for e in range(held):
            xs[e, pl.ds(pl.multiple_of(j * CAP, CAP), CAP)] = got[e * CAP : (e + 1) * CAP]

    def pair(g, k):
        t = g // (k + 1)
        return (1 - t) * g + t * k, (1 - t) * k + t * (g - k - 1)

    def own_stage(k):
        offs = (0, -s, s, -2 * s)
        pairs = [(i, k) for i in range(k)] + [(k, j) for j in range(k)] + [(k, k)]
        for i, j in pairs:
            b = p.slot(offs[i], offs[j], core)
            if j > 1:
                wait_dy(b, 0)
            if i > 1:
                wait_dy(b, 1)
            send_sib(block(b), b)

        def one(g, _):
            i, j = pair(g, k)
            pick_rows(p.slot(p.around(i), p.around(j), core))
            return 0

        lax.fori_loop(0, 2 * k + 1, one, 0)

    def sib_stage(k):
        def one(g, _):
            i, j = pair(g, k)
            b = p.slot(-p.around(i), -p.around(j), 1 - core)
            wait_sib(b)
            pick_rows(b)
            return 0

        lax.fori_loop(0, 2 * k + 1, one, 0)

    local[0].wait()
    pick_rows(p.own)
    own_stage(1)
    sib_stage(0)
    own_stage(2)
    pass_rows(b_via, rw, 1, 0, b_ss, b_rs, lambda c: 2 * s, row_sends[1])
    sib_stage(1)
    own_stage(3)
    sib_stage(2)
    sib_stage(3)

    for c in dys:
        c.wait_send()
    own_rows.wait()

    def others():
        for dc in (0, 1):
            c2 = core if dc == 0 else 1 - core
            for dy in range(NY):
                for dz in range(NZL):
                    if dc or dy or dz:
                        yield p.slot(dy, dz, c2)

    chunk = groups * CAP // 4
    piece = width // NP
    nt = 256
    late = []

    def rows_of(e, x):
        x = lax.rem(x + 2 * NX, NX)
        return pl.ds(pl.multiple_of(e * hid + x * rows, rows), rows)

    def weighted_here(e):
        for j in others():
            a = of_expert(rw, j, e)
            remote(a, a, b_ss.at[e, 0], b_rs.at[e, j], p.dev(1, 0, core)).wait_recv()
        for c in row_sends[e]:
            c.wait_send()
        for i in range(4):
            got = rw[i * 8 : (i + 1) * 8, e * CAP : (e + 1) * CAP].reshape(chunk, hid)
            wt[e, :, i * chunk : (i + 1) * chunk] = got.T

    def to_x(e, h, k, x, dx):
        cols = pl.ds(h * piece, piece)
        src = rdy.at[rows_of(e, x), cols]
        dst = rg.at[k, e, :, cols]
        start(remote(src, dst, e_ss.at[e, h, k], e_rs.at[e, h, k], p.dev_x(dx)), late)

    def from_x(e, h, k):
        a = rg.at[k, e, :, pl.ds(h * piece, piece)]
        remote(a, a, e_ss.at[e, h, k], e_rs.at[e, h, k], p.dev_x(1)).wait_recv()

    def grad_piece(e, h):
        def tile(n, _):
            cols = pl.ds(pl.multiple_of(h * piece + n * nt, nt), nt)
            g = jnp.dot(wt[e], xs[e, :, cols], preferred_element_type=F32)
            rdy[e * hid : (e + 1) * hid, cols] = g.astype(BF)
            g_tile[...] = g
            own_g[e, :, cols] = g_tile[mine_w]
            return 0

        lax.fori_loop(0, piece // nt, tile, 0)
        to_x(e, h, 0, p.x + 2 * s, s)
        to_x(e, h, 1, p.x - s, -s)

    def relay_piece(e, h):
        cols = pl.ds(h * piece, piece)
        from_x(e, h, 0)
        r = rows_of(e, p.x + s)
        rdy[r, cols] = (rdy[r, cols].astype(F32) + rg[0, e, :, cols].astype(F32)).astype(BF)
        to_x(e, h, 2, p.x + s, s)

    back_at = held * hid

    def back_of(e, j, n):
        at_j = pl.multiple_of(back_at + e * groups * CAP + j * CAP, CAP)
        return rdy.at[pl.ds(at_j, n * CAP), pl.ds(0, hid)]

    def back_tile(e, dy):
        yy = lax.rem(p.y + dy + NY, NY)
        x_rows = xs[e, pl.ds(pl.multiple_of(yy * 256, 256), 256)]
        got = lax.dot_general(x_rows, wf[e], (((1,), (1,)), ((), ())), preferred_element_type=F32)
        to = pl.multiple_of(back_at + e * groups * CAP + yy * 256, 256)
        rdy[pl.ds(to, 256), :hid] = got.astype(BF)

    home = peers(p, lambda c: 4 * c - 2)

    def back_rows(e):
        for dy in (2, 1, -1, 0):
            back_tile(e, dy)
            if dy == 2:
                far = back_of(e, lax.rem(p.y + 2, NY) * 2 * NZL, 2 * NZL)
                c = remote(far, d_via.at[e], d_ss.at[e, 31], v_rs.at[1, e], p.dev(s, 0, core))
                start(c, late)
            for k, (dev, dy2) in enumerate(home):
                if dy2 == dy:
                    src, dst = back_of(e, dev["expert"], 1), of_expert(rback, p.own, e)
                    start(remote(src, dst, d_ss.at[e, k], d_rs.at[e, p.own], dev), late)

    def pass_back(e):
        blk = d_via.at[e]
        remote(blk, blk, d_ss.at[e, 31], v_rs.at[1, e], p.dev(s, 0, core)).wait_recv()
        origin = p.slot(-s, 0, core)
        for i, dev in enumerate(far_row(p, s, lambda c: 4 * c - 2)):
            j = lax.rem(dev["expert"], 2 * NZL)
            src = d_via.at[e, pl.ds(pl.multiple_of(j * CAP, CAP), CAP)]
            dst = of_expert(rback, origin, e)
            start(remote(src, dst, d_ss.at[e, 23 + i], d_rs.at[e, origin], dev), late)

    keep = rows // 2

    def to_z(src, dst, k, e, h):
        cols = pl.ds(h * piece, piece)
        c = remote(
            src.at[e, :, cols], dst.at[e, :, cols], z_ss.at[k, e, h], z_rs.at[k, e, h],
            p.dev(0, 2 * s, core),
        )
        start(c, late)

    def from_z(dst, k, e, h):
        a = dst.at[e, :, pl.ds(h * piece, piece)]
        remote(a, a, z_ss.at[k, e, h], z_rs.at[k, e, h], p.dev(0, 2 * s, core)).wait_recv()

    def pass_z(e, h):
        from_z(ez_t, 0, e, h)
        to_z(ez_t, ez_r, 1, e, h)

    def reduce_piece(e, h):
        cols = pl.ds(h * piece, piece)
        from_x(e, h, 1)
        from_x(e, h, 2)

        def total(r):
            at_r = pl.ds(pl.multiple_of(r * keep, keep), keep)
            t = own_g[e, at_r, cols]
            for k in (1, 2):
                t += rg[k, e, at_r, cols].astype(F32)
            return t

        ez_s[e, :, cols] = total(1 - p.half).astype(BF)
        gs_ref[e, :, cols] = total(p.half)
        to_z(ez_s, ez_t, 0, e, h)

    tk = step // top
    sub = lax.broadcasted_iota(jnp.int32, (step, tokens), 0) // top
    lane = lax.broadcasted_iota(jnp.int32, (step, tokens), 1)

    def join(i, _):
        r = pl.ds(pl.multiple_of(i * step, step), step)
        here = sub + i * tk == lane

        def column(rows):
            wide = jnp.broadcast_to(rows[None], (tk, top, tokens)).reshape(step, tokens)
            return jnp.sum(jnp.where(here, wide, jnp.zeros_like(wide)), axis=1, keepdims=True)

        pick = column(slot_t) == lax.broadcasted_iota(jnp.int32, (step, groups * slots), 1)
        got = jnp.dot(
            pick.astype(F32).astype(BF),
            rback[...].reshape(groups * slots, hid),
            preferred_element_type=F32,
        )
        hg_ref[r] = (column(gate_ref[...]) * got).astype(BF)
        dots = jnp.sum(hid_ref[r].astype(F32) * got, axis=1, keepdims=True)
        gg_ref[...] += jnp.sum(
            jnp.where(here, dots, 0.0).reshape(tk, top, tokens), axis=0
        )
        return 0

    def joins(lo, hi):
        lax.fori_loop(lo, hi, join, 0)

    def whole_weights():
        for dx in (1, 2):
            j = lax.rem(p.x + dx * s + 2 * NX, NX)
            remote(shard(j), shard(j), w_ss.at[0], w_rs.at[j], p.dev_x(1)).wait_recv()

    def returned():
        for c in own_back:
            c.wait()
        for j in others():
            for e in range(held):
                a = of_expert(rback, j, e)
                remote(a, a, d_ss.at[e, 0], d_rs.at[e, j], p.dev(1, 0, core)).wait_recv()

    def finish(e, h):
        cols = pl.ds(h * piece, piece)
        from_z(ez_r, 1, e, h)
        gs_ref[e, :, cols] += ez_r[e, :, cols].astype(F32)

    gg_ref[...] = jnp.zeros_like(gg_ref)
    own_back = [
        pltpu.make_async_copy(back_of(e, p.own, 1), of_expert(rback, p.own, e), l_sem.at[2 + e])
        for e in range(held)
    ]
    steps = {
        "g": grad_piece, "r": relay_piece, "R": reduce_piece, "Z": pass_z, "F": finish,
    }
    for word in " ".join(ORDER).split():
        if word[0] in steps:
            steps[word[0]](int(word[1:]) // NP, int(word[1:]) % NP)
        elif word[0] == "W":
            weighted_here(int(word[1]))
        elif word == "V":
            whole_weights()
        elif word[0] == "B":
            back_rows(int(word[1]))
        elif word[0] == "P":
            pass_back(int(word[1]))
        elif word[0] == "O":
            own_back[int(word[1])].start()
        elif word == "D":
            returned()
        elif word[0] == "C":
            joins(int(word[1]), int(word[2]))
    for c in early + late:
        c.wait_send()


def whole(dy, ids_t, hidden, gate_t, wq, we_t):
    tokens, width = dy.shape
    held, rows, _ = wq.shape
    routes, hid = hidden.shape
    groups = lax.axis_size("expert")
    slots = held * CAP
    full = rows * NX
    dma = pltpu.SemaphoreType.DMA
    vm = pltpu.VMEM
    return pl.pallas_call(
        whole_kernel,
        out_shape=(
            jax.ShapeDtypeStruct((routes, hid), BF),
            jax.ShapeDtypeStruct(gate_t.shape, F32),
            jax.ShapeDtypeStruct((held, rows // 2, width), F32),
        ),
        in_specs=[VMEM, VMEM, ANY, VMEM, ANY, VMEM],
        out_specs=(VMEM,) * 3,
        scratch_shapes=[
            vm((groups * tokens, width), BF),
            vm((groups,) + ids_t.shape, jnp.int32),
            vm((groups, slots, hid), BF),
            vm((groups, slots, hid), BF),
            vm((held, full, width), BF),
            vm((held, groups * CAP, width), BF),
            vm((held, hid, groups * CAP), BF),
            vm((held, rows, width), F32),
            vm((NX - 1, held, rows, width), BF),
            vm((groups, slots, hid), BF),
            vm((2 * NZL, slots, hid), BF),
            vm((held, 2 * NZL * CAP, hid), BF),
            vm((held, rows // 2, width), BF),
            vm((held, rows // 2, width), BF),
            vm((held, rows // 2, width), BF),
            vm((held, groups, tokens), F32),
            vm((hid, 256), F32),
            vm((routes, hid), BF),
            vm(wq.shape, BF),
            dma((2, 15)), dma((2, 32)), dma((16,)), dma((32,)), dma((31,)), dma((32,)),
            dma((held, 32)), dma((held, 32)), dma((3,)), dma((4,)), dma((held, 32)), dma((held, 32)),
            dma((held, NP, 3)), dma((held, NP, 3)), dma((2, held)), dma((2, held, NP)), dma((2, held, NP)), dma((6,)),
        ],
        compiler_params=pltpu.CompilerParams(
            has_side_effects=True, vmem_limit_bytes=67043328, collective_id=0
        ),
        name="whole",
    )(dy, ids_t, hidden, gate_t, wq, we_t)


def body(
    out_grad, hidden_saved, gate_probs, expert_ids, weight_q, weight_exp, master, moment1, moment2
):
    tokens, top = expert_ids.shape
    hid = hidden_saved.shape[2]
    routes = tokens * top

    hidden_grad, gate_grad, gradient = whole(
        out_grad,
        expert_ids.T,
        hidden_saved.reshape(routes, hid),
        gate_probs.T,
        weight_q,
        weight_exp.transpose(0, 2, 1),
    )
    first = 0.9 * moment1.astype(F32) + 0.1 * gradient
    second = 0.95 * moment2.astype(F32) + 0.05 * gradient * gradient
    update = first / (1.0 - 0.9**20) / (jnp.sqrt(second / (1.0 - 0.95**20)) + 1e-08) + 0.1 * master
    return (
        hidden_grad.reshape(tokens, top, hid),
        gate_grad.T,
        master - 0.001 * update,
        first.astype(BF),
        second.astype(BF),
    )


def solution(mesh):
    tok = ("expert", "fsdp", "replica")
    in_specs = (
        P(tok, None),
        P(tok, None, None),
        P(tok, None),
        P(tok, None),
        P("expert", "fsdp", None),
        P("expert", "fsdp", None),
        P("expert", ("fsdp", "replica"), None),
        P("expert", ("fsdp", "replica"), None),
        P("expert", ("fsdp", "replica"), None),
    )
    out_specs = (
        P(tok, None, None),
        P(tok, None),
        P("expert", ("fsdp", "replica"), None),
        P("expert", ("fsdp", "replica"), None),
        P("expert", ("fsdp", "replica"), None),
    )
    return jax.shard_map(body, mesh=mesh, in_specs=in_specs, out_specs=out_specs, check_vma=False)
```
